32 devices in a mesh: batch: 2 (over x), ctx: 4 (over y, core), mp: 4 (over z).
Axes of the slice: x: 2, y: 2, z: 4, core: 2. Of those that a mesh axis runs over, the one named last changes fastest.
Arguments:
- hidden_in: bfloat16 [4, 512, 1024], P('batch', 'ctx'), may hold values from -6 to 6
- segment_ids: int32 [4, 512], P('batch', 'ctx'), may hold values from 0 to 3, never falling along the last dimension, each value on 1 to 256 neighbouring positions
- gains: bfloat16 [2, 2, 1024], P(None, None, ('batch', 'ctx', 'mp')), may hold values from 0.5 to 1.5
- biases: bfloat16 [2, 10, 1024], P(None, None, ('batch', 'ctx', 'mp')), may hold values from -3 to 3
- w_qkv: bfloat16 [2, 1024, 3, 1024], P(None, ('batch', 'ctx'), None, 'mp'), may hold values from -0.1875 to 0.1875
- w_out_t: bfloat16 [2, 1024, 1024], P(None, ('batch', 'ctx'), 'mp'), may hold values from -0.5 to 0.5
- w_up: bfloat16 [2, 1024, 4096], P(None, ('batch', 'ctx'), 'mp'), may hold values from -0.1875 to 0.1875
- w_down_t: bfloat16 [2, 1024, 4096], P(None, ('batch', 'ctx'), 'mp'), may hold values from -0.09375 to 0.09375
- grad_out: bfloat16 [4, 512, 1024], P('batch', 'ctx'), may hold values from -6 to 6
Outputs:
- output: bfloat16 [4, 512, 1024], P('batch', 'ctx')
- grad_in: bfloat16 [4, 512, 1024], P('batch', 'ctx')
- grad_gains: float32 [2, 2, 1024], P(None, None, ('batch', 'ctx', 'mp'))
- grad_biases: float32 [2, 10, 1024], P(None, None, ('batch', 'ctx', 'mp'))
- grad_qkv: float32 [2, 1024, 3, 1024], P(None, ('batch', 'ctx'), None, 'mp')
- grad_attn_out: float32 [2, 1024, 1024], P(None, ('batch', 'ctx'), 'mp')
- grad_up: float32 [2, 1024, 4096], P(None, ('batch', 'ctx'), 'mp')
- grad_down: float32 [2, 1024, 4096], P(None, ('batch', 'ctx'), 'mp')
The draws below stay inside these ranges and needn't reach their ends.
Inputs may be any that keep to these rules, and one draw needn't show every extreme that they name: `segment_ids`: document numbers never fall along a sequence; every document spans 1 to 256 tokens, and one of each sequence spans exactly that many.
All inputs are finite; a program needn't handle non-finite values.
Results may differ from the reference program's by a relative error of at most 0.023.
Values may be sent and summed in bfloat16 or wider, within the bound.
A program may use at most 128 MiB of HBM per device.

```python
import math
import jax
import jax.numpy as jnp
import numpy as np
from jax import lax

MODEL_WIDTH = 1024
HEADS = 16
HEAD = 64
FF = 4096
LAYERS = 2
SEQUENCES = 4
LENGTH = 512


def shard_levels(own_key, extent, cuts, smallest, largest):
    def one(position, parts):
        heights = jax.random.uniform(jax.random.fold_in(jax.random.fold_in(own_key, 6), position), (parts,), jnp.float32, smallest / len(cuts), largest / len(cuts))
        return jnp.repeat(jnp.exp(heights), extent[position] // parts).reshape((-1,) + (1,) * (len(extent) - position - 1))

    loudness = one(*cuts[0])
    for cut in cuts[1:]:
        loudness = loudness * one(*cut)
    return loudness


def length_profile(number_of, total, most, skew):
    loads = [(1 << 20) // math.isqrt(grade ** skew) + 1 for grade in range(2, number_of + 1)]
    rest, given = total - most - (number_of - 1), [1] * (number_of - 1)
    while rest > 0:
        free = [i for i in range(number_of - 1) if given[i] < most]
        pool, left = sum([loads[i] for i in free]), rest
        for i in free:
            extra = min(most - given[i], max(1, left * loads[i] // pool), rest)
            given[i] = given[i] + extra
            rest = rest - extra
    return np.array([most] + given)


def ragged(rng, count, total, reach, skew):
    if count == 2:
        one = jax.random.randint(rng, (), max(1, total - reach), min(reach, total - 1) + 1)
        return jnp.stack([one, total - one])
    tallies = jnp.asarray(length_profile(count, total, reach, skew), jnp.int32)
    couples = (count - 1) // 2
    source_of, sink = tallies[1:1 + 2 * couples:2], tallies[2:2 + 2 * couples:2]
    margin = jnp.minimum(source_of - 1, reach - sink)
    moved = jax.random.randint(jax.random.fold_in(rng, 1), (couples,), 0, 1 << 20) % (margin + 1)
    tallies = tallies.at[1:1 + 2 * couples:2].set(source_of - moved).at[2:2 + 2 * couples:2].set(sink + moved)
    return tallies[jax.random.permutation(jax.random.fold_in(rng, 2), count)]


def scatter_about(key, shape, scale, bound, cuts=(), held_as=jnp.bfloat16):
    factor_of = shard_levels(key, shape, cuts, -0.22, 0.18) if cuts else 1.0
    result = jax.random.normal(key, shape, jnp.float32) * scale * factor_of
    return jnp.minimum(jnp.maximum(result, -bound), bound).astype(held_as)


def setup_inputs(seed: int = 0) -> dict:
    streams_of = jax.random.split(jax.random.key(seed), 10)
    hidden_in = scatter_about(streams_of[0], (SEQUENCES, LENGTH, MODEL_WIDTH), 1.0, 6.0, ((0, 2), (1, 4)))
    segment_ids = jax.vmap(lambda own: jnp.searchsorted(jnp.cumsum(ragged(own, max(3, LENGTH // 128), LENGTH, LENGTH // 2, 2)), jnp.arange(LENGTH), side="right"))(jax.random.split(streams_of[1], SEQUENCES)).reshape((SEQUENCES, LENGTH)).astype(jnp.int32)
    gains = jnp.clip(1.0 + 0.1 * jax.random.normal(streams_of[2], (LAYERS, 2, MODEL_WIDTH), jnp.float32), 0.5, 1.5).astype(jnp.bfloat16)
    biases = scatter_about(streams_of[3], (LAYERS, 10, MODEL_WIDTH), 0.5, 3.0, ((2, 32),))
    w_qkv = scatter_about(streams_of[4], (LAYERS, MODEL_WIDTH, 3, MODEL_WIDTH), MODEL_WIDTH ** -0.5, 0.1875, ((1, 8), (3, 4)))
    w_out_t = scatter_about(streams_of[5], (LAYERS, MODEL_WIDTH, MODEL_WIDTH), (MODEL_WIDTH // 8) ** -0.5, 0.5, ((1, 8), (2, 4)))
    w_up = scatter_about(streams_of[6], (LAYERS, MODEL_WIDTH, FF), MODEL_WIDTH ** -0.5, 0.1875, ((1, 8), (2, 4)))
    w_down_t = scatter_about(streams_of[7], (LAYERS, MODEL_WIDTH, FF), FF ** -0.5, 0.09375, ((1, 8), (2, 4)))
    grad_out = scatter_about(streams_of[8], (SEQUENCES, LENGTH, MODEL_WIDTH), 1.0, 6.0, ((0, 2), (1, 4)))
    return dict(hidden_in=hidden_in, segment_ids=segment_ids, gains=gains, biases=biases, w_qkv=w_qkv, w_out_t=w_out_t, w_up=w_up, w_down_t=w_down_t, grad_out=grad_out)


EPS = 1e-05
GELU_C = 0.7978845608028654
GELU_K = 0.044715

def rounded(values):
    return lax.optimization_barrier(values.astype(jnp.bfloat16)).astype(jnp.float32)

def norm_parts(values):
    center = values - lax.optimization_barrier(jnp.mean(values, -1, keepdims=True))
    inverse = lax.rsqrt(lax.optimization_barrier(jnp.mean(center * center, -1, keepdims=True)) + EPS)
    return (center * inverse, inverse)

def norm_back(grad_y, normed, inverse, gain):
    scaled = grad_y * gain
    return inverse * (scaled - lax.optimization_barrier(jnp.mean(scaled, -1, keepdims=True)) - normed * lax.optimization_barrier(jnp.mean(scaled * normed, -1, keepdims=True)))

def gelu_parts(values):
    bend = jnp.tanh(GELU_C * (values + GELU_K * values * values * values))
    return (0.5 * values * (1.0 + bend), bend)

def gelu_slope(values, bend):
    return 0.5 * (1.0 + bend) + 0.5 * values * (1.0 - bend * bend) * GELU_C * (1.0 + 3.0 * GELU_K * values * values)

def attention_rows(query, keys, seg, start, slope):
    rows = query.shape[0]
    length = keys.shape[0]
    q_pos = start + jnp.arange(rows, dtype=jnp.int32)
    k_pos = jnp.arange(length, dtype=jnp.int32)
    q_seg = lax.dynamic_slice_in_dim(seg, start, rows, 0)
    mask = (k_pos[None, :] <= q_pos[:, None]) & (seg[None, :] == q_seg[:, None])
    dist = (q_pos[:, None] - k_pos[None, :]).astype(jnp.float32)
    scale = 1.0 / math.sqrt(HEAD)
    score = jnp.einsum('qhd,khd->hqk', query.astype(jnp.float32), keys.astype(jnp.float32)) * scale - slope[:, None, None] * dist[None]
    return (score, mask[None])

def attention_forward(query_key_value, seg, slope):
    length = query_key_value.shape[0]
    rows = min(512, length)

    def one(index):
        start = index * rows
        query = lax.dynamic_slice_in_dim(query_key_value[:, 0], start, rows, 0)
        score, mask = attention_rows(query, query_key_value[:, 1], seg, start, slope)
        expo = jnp.where(mask, jnp.exp(jnp.where(mask, score, 0.0)), 0.0)
        total = lax.optimization_barrier(jnp.sum(expo, -1))
        summed = jnp.einsum('hqk,khd->qhd', rounded(expo), query_key_value[:, 2].astype(jnp.float32))
        out = summed / jnp.transpose(total)[:, :, None]
        return (out.astype(jnp.bfloat16), jnp.log(total))
    outs, lses = lax.map(one, jnp.arange(length // rows, dtype=jnp.int32))
    return (outs.reshape(length, HEADS, HEAD), jnp.transpose(lses, (1, 0, 2)).reshape(HEADS, length))

def attention_backward(query_key_value, seg, ctx, lse, dctx, slope):
    length = query_key_value.shape[0]
    rows = min(512, length)
    scale = 1.0 / math.sqrt(HEAD)
    keys = query_key_value[:, 1].astype(jnp.float32)
    values = query_key_value[:, 2].astype(jnp.float32)

    def step(carry, index):
        dkey, dvalue = carry
        start = index * rows
        query = lax.dynamic_slice_in_dim(query_key_value[:, 0], start, rows, 0)
        score, mask = attention_rows(query, query_key_value[:, 1], seg, start, slope)
        lse_rows = lax.dynamic_slice_in_dim(lse, start, rows, 1)
        prob = jnp.where(mask, jnp.exp(jnp.where(mask, score - lse_rows[:, :, None], 0.0)), 0.0)
        dctx_rows = lax.dynamic_slice_in_dim(dctx, start, rows, 0).astype(jnp.float32)
        ctx_rows = lax.dynamic_slice_in_dim(ctx, start, rows, 0).astype(jnp.float32)
        dvalue = dvalue + jnp.einsum('hqk,qhd->khd', rounded(prob), dctx_rows)
        dprob = jnp.einsum('qhd,khd->hqk', dctx_rows, values)
        delta = jnp.transpose(lax.optimization_barrier(jnp.sum(dctx_rows * ctx_rows, -1)))
        dscore = rounded(prob * (dprob - delta[:, :, None]))
        dquery = jnp.einsum('hqk,khd->qhd', dscore, keys) * scale
        dkey = dkey + jnp.einsum('hqk,qhd->khd', dscore, query.astype(jnp.float32)) * scale
        return ((dkey, dvalue), dquery)
    zeros = jnp.zeros((length, HEADS, HEAD), jnp.float32)
    (dkey, dvalue), dquery = lax.scan(step, (zeros, zeros), jnp.arange(length // rows, dtype=jnp.int32))
    return (dquery.reshape(length, HEADS, HEAD), dkey, dvalue)

def layer_forward(x, gain, bias, wqkv, wout, wup, wdown, seg, slope):
    normed1, inverse1 = norm_parts(x)
    first_activation = (normed1 * gain[0] + bias[0]).astype(jnp.bfloat16)
    query_key_value = jnp.dot(first_activation.reshape(-1, MODEL_WIDTH), wqkv.reshape(MODEL_WIDTH, 3 * MODEL_WIDTH), preferred_element_type=jnp.float32).reshape(-1, 3, MODEL_WIDTH)
    shift = jnp.stack([bias[2], jnp.zeros_like(bias[2]), bias[3]])
    heads = (query_key_value + shift).astype(jnp.bfloat16).reshape(SEQUENCES, LENGTH, 3, HEADS, HEAD)
    ctx, lse = lax.map(lambda pair: attention_forward(pair[0], pair[1], slope), (heads, seg))
    attn = jnp.dot(ctx.reshape(-1, MODEL_WIDTH), wout.T, preferred_element_type=jnp.float32).reshape(x.shape)
    x2 = x + attn + bias[4]
    normed2, inverse2 = norm_parts(x2)
    second_activation = (normed2 * gain[1] + bias[1]).astype(jnp.bfloat16)
    up_projected = jnp.dot(second_activation.reshape(-1, MODEL_WIDTH), wup, preferred_element_type=jnp.float32) + bias[6:].reshape(FF)
    act, bend = gelu_parts(up_projected)
    act_bf = act.astype(jnp.bfloat16)
    down = jnp.dot(act_bf, wdown.T, preferred_element_type=jnp.float32).reshape(x.shape)
    return (x2 + down + bias[5], (x, first_activation, heads, ctx, lse, x2, second_activation, up_projected, act_bf))

def layer_backward(saved, grad_y, gain, bias, wqkv, wout, wup, wdown, seg, slope):
    x, first_activation, heads, ctx, lse, x2, second_activation, up_projected, act_bf = saved
    grad_flat = grad_y.reshape(-1, MODEL_WIDTH)
    grad_bf = grad_flat.astype(jnp.bfloat16)
    grad_bd = lax.optimization_barrier(jnp.sum(grad_flat, 0))
    grad_wd = jnp.dot(grad_bf.T, act_bf, preferred_element_type=jnp.float32)
    dact = jnp.dot(grad_bf, wdown, preferred_element_type=jnp.float32)
    _, bend = gelu_parts(up_projected)
    dup = dact * gelu_slope(up_projected, bend)
    grad_bu = lax.optimization_barrier(jnp.sum(dup, 0))
    up_gradient_half_precision = dup.astype(jnp.bfloat16)
    up_weight_gradient = jnp.dot(second_activation.reshape(-1, MODEL_WIDTH).T, up_gradient_half_precision, preferred_element_type=jnp.float32)
    da2 = jnp.dot(up_gradient_half_precision, wup.T, preferred_element_type=jnp.float32)
    normed2, inverse2 = norm_parts(x2.reshape(-1, MODEL_WIDTH))
    grad_g2 = lax.optimization_barrier(jnp.sum(da2 * normed2, 0))
    grad_b2 = lax.optimization_barrier(jnp.sum(da2, 0))
    gx2 = grad_flat + norm_back(da2, normed2, inverse2, gain[1])
    grad_bo = lax.optimization_barrier(jnp.sum(gx2, 0))
    gx2_bf = gx2.astype(jnp.bfloat16)
    grad_wo = jnp.dot(gx2_bf.T, ctx.reshape(-1, MODEL_WIDTH), preferred_element_type=jnp.float32)
    dctx = jnp.dot(gx2_bf, wout, preferred_element_type=jnp.float32).astype(jnp.bfloat16).reshape(SEQUENCES, LENGTH, HEADS, HEAD)
    dq, dk, value_gradient = lax.map(lambda item: attention_backward(item[0], item[1], item[2], item[3], item[4], slope), (heads, seg, ctx, lse, dctx))
    query_gradient_flat = dq.reshape(-1, MODEL_WIDTH)
    key_gradient_flat = dk.reshape(-1, MODEL_WIDTH)
    value_gradient_flat = value_gradient.reshape(-1, MODEL_WIDTH)
    grad_bq = lax.optimization_barrier(jnp.sum(query_gradient_flat, 0))
    value_bias_gradient = lax.optimization_barrier(jnp.sum(value_gradient_flat, 0))
    packed_projection_gradient = jnp.stack([query_gradient_flat, key_gradient_flat, value_gradient_flat], 1).astype(jnp.bfloat16).reshape(-1, 3 * MODEL_WIDTH)
    grad_wqkv = jnp.dot(first_activation.reshape(-1, MODEL_WIDTH).T, packed_projection_gradient, preferred_element_type=jnp.float32).reshape(MODEL_WIDTH, 3, MODEL_WIDTH)
    da1 = jnp.dot(packed_projection_gradient, wqkv.reshape(MODEL_WIDTH, 3 * MODEL_WIDTH).T, preferred_element_type=jnp.float32)
    normed1, inverse1 = norm_parts(x.reshape(-1, MODEL_WIDTH))
    grad_g1 = lax.optimization_barrier(jnp.sum(da1 * normed1, 0))
    grad_b1 = lax.optimization_barrier(jnp.sum(da1, 0))
    grad_x = gx2 + norm_back(da1, normed1, inverse1, gain[0])
    grad_gain = jnp.stack([grad_g1, grad_g2])
    grad_bias = jnp.concatenate([jnp.stack([grad_b1, grad_b2, grad_bq, value_bias_gradient, grad_bo, grad_bd]), grad_bu.reshape(FF // MODEL_WIDTH, MODEL_WIDTH)], 0)
    return (grad_x.reshape(grad_y.shape), grad_gain, grad_bias, grad_wqkv, grad_wo, up_weight_gradient, grad_wd)

def reference(hidden_in, segment_ids, gains, biases, w_qkv, w_out_t, w_up, w_down_t, grad_out):
    slope = jnp.exp2(-8.0 * (jnp.arange(HEADS, dtype=jnp.int32).astype(jnp.float32) + 1.0) / HEADS)
    state = hidden_in.astype(jnp.float32)
    saves = []
    for layer in range(LAYERS):
        state, saved = layer_forward(state, gains[layer], biases[layer], w_qkv[layer], w_out_t[layer], w_up[layer], w_down_t[layer], segment_ids, slope)
        saves.append(saved)
    output = state.astype(jnp.bfloat16)
    grad = grad_out.astype(jnp.float32)
    results = []
    for layer in reversed(range(LAYERS)):
        outcome = layer_backward(saves[layer], grad, gains[layer], biases[layer], w_qkv[layer], w_out_t[layer], w_up[layer], w_down_t[layer], segment_ids, slope)
        grad = outcome[0]
        results.insert(0, outcome[1:])
    grad_gains = jnp.stack([item[0] for item in results])
    grad_biases = jnp.stack([item[1] for item in results])
    grad_qkv = jnp.stack([item[2] for item in results])
    grad_attn_out = jnp.stack([item[3] for item in results])
    grad_up = jnp.stack([item[4] for item in results])
    grad_down = jnp.stack([item[5] for item in results])
    return (output, grad.astype(jnp.bfloat16), grad_gains, grad_biases, grad_qkv, grad_attn_out, grad_up, grad_down)
```

```python
import math

import jax
import jax.numpy as jnp
from jax import lax
from jax.experimental import pallas as pl
from jax.experimental.pallas import tpu as pltpu
from jax.sharding import PartitionSpec as P

HEADS = 16
HEAD = 64
EPS = 1e-05
GELU_C = 0.7978845608028654
GELU_K = 0.044715
LANES = 128
VEC_ROWS = 32
CHUNK = 32
LAG = 2
F32 = jnp.float32
BF16 = jnp.bfloat16

MESH = pl.DeviceIdType.MESH
ANY = pl.BlockSpec(memory_space=pl.ANY)
VMEM = pl.BlockSpec(memory_space=pltpu.VMEM)


def nn(a, b):
    return lax.dot_general(a, b, (((1,), (0,)), ((), ())), preferred_element_type=F32)


def nt(a, b):
    return lax.dot_general(a, b, (((1,), (1,)), ((), ())), preferred_element_type=F32)


def tn(a, b):
    return lax.dot_general(a, b, (((0,), (0,)), ((), ())), preferred_element_type=F32)


def norm_parts(values):
    center = values - jnp.mean(values, -1, keepdims=True)
    inverse = lax.rsqrt(jnp.mean(center * center, -1, keepdims=True) + EPS)
    return center * inverse, inverse


def norm_back(grad_y, normed, inverse, gain):
    scaled = grad_y * gain
    return inverse * (
        scaled
        - jnp.mean(scaled, -1, keepdims=True)
        - normed * jnp.mean(scaled * normed, -1, keepdims=True)
    )


def device_at(kind, rank):
    if kind in ("mp", "ctx"):
        return {kind: rank}
    count = lax.axis_size("ctx")
    return {"batch": rank // count, "ctx": lax.rem(rank, count)}


def remote(src, dst, send, recv, device):
    return pltpu.make_async_remote_copy(
        src_ref=src, dst_ref=dst, send_sem=send, recv_sem=recv,
        device_id=device, device_id_type=MESH,
    )


def colsum(values):
    return jnp.sum(values, 0, keepdims=True)


def run_all(x0, gout, seg, seg_t, vec, weights, dims):
    (layers, seqs, rows, width, cols, ffc, part, owners, ctx_count, mp_count, steps) = dims
    tokens = seqs * rows
    chips = owners // 2
    piece = width // owners
    heads = cols // HEAD
    stack = heads * rows
    back = (ctx_count * rows // 2 + rows - 2) // rows
    chunks = tokens // CHUNK
    sizes = [w.shape[2] for w in weights]
    tiles = width // LANES
    group = owners // tiles
    backward_on = steps

    def kernel(
        x0_ref, go_ref, seg_ref, segt_ref, vec_ref, wq_in, wo_in, wu_in, wd_in,
        out_ref, gin_ref, term_out, rq, ro, ru, rd,
        wq, wo, wu, wd, x1, x2, a1, qkv, kvl, ctxs, lse, a2, gs, act,
        part_b, out_a, out_b, land_a, land_b, gy, gyb, dub, dctx, dqkv, dkv0,
        dkv_out, dkv_in, gq, gw, gu, gd, cq, co, cu, cd,
        vz, vland, vsum, vecs, kseg, term, tland, tsum, tz, acc, qst, dst,
        loc_sem, wsend, wrecv, fsend, frecv, asend, arecv, bsend, brecv,
        vsend, vrecv, v2send, v2recv, ksend, krecv, gsend, grecv, dsend, drecv,
        csend, crecv, hsend, hrecv, own_sem, t1send, t1recv, t2send, t2recv,
    ):
        me = lax.axis_index("mp")
        here = lax.axis_index("ctx")
        rank = lax.axis_index("batch") * ctx_count + here
        chip = rank // 2
        core = lax.rem(rank, 2)
        sib_rank = chip * 2 + 1 - core
        sibling = device_at("flat", sib_rank)
        side = device_at("mp", me + 1 - 2 * lax.rem(me, 2))
        across = device_at("mp", mp_count - 1 - me)
        is_mid = (me == 1) | (me == 2)
        is_end = (me == 0) | (me == 3)
        zpeers = [device_at("mp", lax.rem(me + t, mp_count)) for t in range(1, mp_count)]
        plane = [device_at("flat", lax.rem(rank + t, owners)) for t in range(1, owners)]
        chip_to = [lax.rem(chip + t, chips) * 2 + core for t in range(1, chips)]
        chip_from = [lax.rem(chip + chips - t, chips) * 2 + core for t in range(1, chips)]
        w_in = [wq_in, wo_in, wu_in, wd_in]
        w_all = [wq, wo, wu, wd]

        def prow(g):
            return pl.ds(pl.multiple_of(g * piece, piece), piece)

        def crow(c):
            return pl.ds(pl.multiple_of(c * CHUNK, CHUNK), CHUNK)

        def srow(s):
            return pl.ds(s * rows, rows)

        def own_copy(l, m):
            return pltpu.make_async_copy(
                w_in[m].at[l], w_all[m].at[l, prow(rank)], loc_sem.at[l, m]
            )

        def w_copy(l, m, t, g):
            return remote(
                w_in[m].at[l], w_all[m].at[l, prow(g)],
                wsend.at[l, m, t], wrecv.at[l, m, t], device_at("flat", chip_to[t]),
            )

        def f_copy(l, m, t, g):
            src = w_in[m].at[l] if t == 0 else w_all[m].at[l, prow(g)]
            return remote(
                src, w_all[m].at[l, prow(g)], fsend.at[l, m, t], frecv.at[l, m, t], sibling
            )

        def w_issue(l, m):
            for t in range(chips - 1):
                w_copy(l, m, t, rank).start()
            f_copy(l, m, 0, rank).start()
            own_copy(l, m).start()

        def w_forward(l, m):
            for t in range(chips - 1):
                w_copy(l, m, t, chip_from[t]).wait_recv()
                f_copy(l, m, t + 1, chip_from[t]).start()

        def w_ready(l, m):
            own_copy(l, m).wait()
            f_copy(l, m, 0, sib_rank).wait_recv()
            for t in range(chips - 1):
                f_copy(l, m, t + 1, chip_from[t] + 1 - 2 * core).wait_recv()

        barrier = pltpu.get_barrier_semaphore()
        for device in zpeers + plane:
            pl.semaphore_signal(barrier, inc=1, device_id=device, device_id_type=MESH)
        pl.semaphore_wait(barrier, len(zpeers) + len(plane))

        def vz_copy(t):
            return remote(vec_ref, vz.at[t], vsend.at[t], vrecv.at[t], zpeers[t])

        for t in range(mp_count - 1):
            vz_copy(t).start()
        w_issue(0, 0)
        w_issue(0, 1)

        def seg_copy(d):
            return remote(
                seg_ref, kseg.at[d - 1], ksend.at[layers, d - 1, 0], krecv.at[layers, d - 1, 0],
                device_at("ctx", lax.rem(here + d, ctx_count)),
            )

        for d in range(1, back + 1):
            @pl.when(here + d < ctx_count)
            def _():
                seg_copy(d).start()

            @pl.when(here - d < 0)
            def _():
                kseg[d - 1] = jnp.full(kseg.shape[1:], -1, jnp.int32)
                for l in range(layers):
                    kvl[l, d - 1] = jnp.zeros(kvl.shape[2:], BF16)

        vtot = vec_ref[...].astype(F32)
        for t in range(mp_count - 1):
            vz_copy(t).wait_recv()
            vtot = vtot + vz[t].astype(F32)
        vsum[...] = vtot.astype(BF16)

        def v2_copy(t, g):
            return remote(vsum, vland.at[g], v2send.at[t], v2recv.at[t], plane[t])

        for t in range(owners - 1):
            v2_copy(t, rank).start()
        vland[rank] = vsum[...]
        for t in range(owners - 1):
            v2_copy(t, lax.rem(rank + owners - 1 - t, owners)).wait_recv()
        for t in range(tiles):
            tile = vland[t * group].astype(F32)
            for j in range(1, group):
                tile = tile + vland[t * group + j].astype(F32)
            vecs[:, t * LANES : (t + 1) * LANES] = tile
        term[...] = jnp.zeros(term.shape, F32)
        for d in range(1, back + 1):
            @pl.when(here - d >= 0)
            def _():
                seg_copy(d).wait_recv()

        mine = pl.ds(pl.multiple_of(me * cols, LANES), cols)

        def gain_row(l, i):
            return l * 2 + i

        def bias_row(l, j):
            return layers * 2 + l * 10 + j

        def vrow(r):
            return vecs[r : r + 1, :]

        lane_head = lax.broadcasted_iota(jnp.int32, (rows, cols), 1) // HEAD
        head_lanes = [lane_head == h for h in range(heads)]
        row_i = lax.broadcasted_iota(jnp.int32, (rows, rows), 0)
        col_j = lax.broadcasted_iota(jnp.int32, (rows, rows), 1)
        slopes = [
            jnp.exp2(
                jnp.full((1, rows), -8.0 / HEADS, F32)
                * (me * heads + (h + 1)).astype(F32)
            )
            for h in range(heads)
        ]

        def stacked(ref, values):
            for h in range(heads):
                ref[h * rows : (h + 1) * rows, :] = jnp.where(
                    head_lanes[h], values, jnp.zeros_like(values)
                )

        def block_mask(s, d):
            keys = (seg_ref if d == 0 else kseg.at[d - 1])[s : s + 1, :]
            mask = segt_ref[:, s : s + 1] == keys
            return mask & (col_j <= row_i) if d == 0 else mask

        def block_dist(d):
            return (d * rows + row_i - col_j).astype(F32)

        def key_block(l, s, d):
            if d == 0:
                return qkv[l, srow(s), cols : 2 * cols], qkv[l, srow(s), 2 * cols : 3 * cols]
            return kvl[l, d - 1, srow(s), :cols], kvl[l, d - 1, srow(s), cols:]

        def side_copy(p, c, src):
            return remote(
                src.at[p, crow(c)], land_a.at[p, crow(c)], asend.at[p, c], arecv.at[p, c], side
            )

        def cross_copy(p, c):
            return remote(
                out_b.at[p, crow(c)], land_b.at[p, crow(c)], bsend.at[p, c], brecv.at[p, c], across
            )

        counter = [0]

        def sum_drain(p):
            def body(c, carry):
                side_copy(p, c, part_b).wait_send()

                @pl.when(is_mid)
                def _():
                    cross_copy(p, c).wait_send()

                return carry

            lax.fori_loop(0, chunks, body, 0)

        def sum_begin():
            k = counter[0]
            counter[0] += 1
            if k >= 2:
                sum_drain(k % 2)
            return k % 2

        def sum_send(p, low, high):
            @pl.when(is_end)
            def _():
                def body(c, carry):
                    side_copy(p, c, part_b).start()
                    return carry

                lax.fori_loop(low, high, body, 0)

        def sum_finish(p, consumer, filler=None):
            @pl.when(is_mid)
            def _():
                def body(c, carry):
                    @pl.when(c < chunks)
                    def _():
                        side_copy(p, c, part_b).wait_recv()
                        pair = part_b[p, crow(c)].astype(F32) + land_a[p, crow(c)].astype(F32)
                        out_b[p, crow(c)] = pair.astype(BF16)
                        cross_copy(p, c).start()

                    @pl.when(c >= LAG)
                    def _():
                        o = c - LAG
                        cross_copy(p, o).wait_recv()
                        total = out_b[p, crow(o)].astype(F32) + land_b[p, crow(o)].astype(F32)
                        out_a[p, crow(o)] = total.astype(BF16)
                        side_copy(p, o, out_a).start()
                        consumer(o, total.astype(BF16).astype(F32))

                    if filler is not None:
                        @pl.when(c < chunks)
                        def _():
                            filler(c)

                    return carry

                lax.fori_loop(0, chunks + LAG, body, 0)

            @pl.when(is_end)
            def _():
                if filler is not None:
                    def fill(c, carry):
                        filler(c)
                        return carry

                    lax.fori_loop(0, chunks, fill, 0)

                def body(c, carry):
                    side_copy(p, c, part_b).wait_recv()
                    consumer(c, land_a[p, crow(c)].astype(F32))
                    return carry

                lax.fori_loop(0, chunks, body, 0)

        def product_nt(p, left, weight, wide):
            for s in range(seqs):
                def body(t, carry):
                    off = pl.ds(pl.multiple_of(t * 256, 256), 256)
                    part_b[p, srow(s), off] = nt(left[srow(s), :], weight[off, :]).astype(BF16)
                    return carry

                lax.fori_loop(0, wide // 256, body, 0)
                sum_send(p, s * rows // CHUNK, (s + 1) * rows // CHUNK)

        def kv_copy(l, s, d):
            return remote(
                qkv.at[l, srow(s), pl.ds(cols, 2 * cols)], kvl.at[l, d - 1, srow(s)],
                ksend.at[l, d - 1, s], krecv.at[l, d - 1, s],
                device_at("ctx", lax.rem(here + d, ctx_count)),
            )

        def first_norm(l, rws, x):
            normed, _ = norm_parts(x)
            a1[l, rws] = (normed * vrow(gain_row(l, 0)) + vrow(bias_row(l, 0))).astype(BF16)

        def start_norm(c, carry):
            first_norm(0, crow(c), x0_ref[crow(c)].astype(F32))
            return carry

        lax.fori_loop(0, chunks, start_norm, 0)
        w_forward(0, 0)
        w_ready(0, 0)

        def forward_layer(l):
            for u in (1, 2, 0):
                value = nn(a1[l], wq[l, :, u * cols : (u + 1) * cols])
                if u != 1:
                    value = value + vecs[
                        bias_row(l, 2 if u == 0 else 3) : bias_row(l, 2 if u == 0 else 3) + 1, mine
                    ]
                qkv[l, :, u * cols : (u + 1) * cols] = value.astype(BF16)
                if u == 2:
                    for s in range(seqs):
                        for d in range(1, back + 1):
                            @pl.when(here + d < ctx_count)
                            def _():
                                kv_copy(l, s, d).start()
                    w_issue(l, 2)
                    w_issue(l, 3)
            w_forward(l, 1)
            for s in range(seqs):
                stacked(qst, qkv[l, srow(s), :cols] * BF16(1.0 / math.sqrt(HEAD)))
                totals = [jnp.zeros((rows, 1), F32)] * heads
                for d in range(back + 1):
                    if d:
                        @pl.when(here - d >= 0)
                        def _():
                            kv_copy(l, s, d).wait_recv()
                    keys, values = key_block(l, s, d)
                    score = nt(qst[...], keys)
                    mask, dist = block_mask(s, d), block_dist(d)
                    expos = []
                    for h in range(heads):
                        raw = score[h * rows : (h + 1) * rows] - slopes[h] * dist
                        expo = jnp.where(mask, jnp.exp(jnp.where(mask, raw, 0.0)), 0.0)
                        totals[h] = totals[h] + jnp.sum(expo, -1, keepdims=True)
                        expos.append(expo.astype(BF16))
                    step = nn(jnp.concatenate(expos, 0), values)
                    acc[...] = step if d == 0 else acc[...] + step
                out = jnp.zeros((rows, cols), F32)
                for h in range(heads):
                    lse[l * seqs + s, h * rows : (h + 1) * rows, :] = jnp.log(totals[h])
                    out = jnp.where(head_lanes[h], acc[h * rows : (h + 1) * rows, :] / totals[h], out)
                ctxs[l, srow(s)] = out.astype(BF16)
            w_ready(l, 1)
            p = sum_begin()
            product_nt(p, ctxs.at[l], wo.at[l], width)

            def mid_norm(c, total):
                base = x0_ref[crow(c)].astype(F32) if l == 0 else x1[crow(c)]
                value = base + total + vrow(bias_row(l, 4))
                x2[l, crow(c)] = value
                normed, _ = norm_parts(value)
                a2[l, crow(c)] = (
                    normed * vrow(gain_row(l, 1)) + vrow(bias_row(l, 1))
                ).astype(BF16)

            sum_finish(p, mid_norm)
            w_forward(l, 2)
            w_forward(l, 3)
            if l + 1 < layers:
                w_issue(l + 1, 0)
                w_issue(l + 1, 1)
            w_ready(l, 2)

            def up_tile(t, carry):
                off = pl.ds(pl.multiple_of(t * 256, 256), 256)
                up = nn(a2[l], wu[l, :, off]) + vecs[pl.ds(bias_row(l, 6) + me, 1), off]
                square = up * up
                bend = jnp.tanh(GELU_C * (up + GELU_K * square * up))
                half = 0.5 * (1.0 + bend)
                act[l, :, off] = (up * half).astype(BF16)
                gs[l, :, off] = half + 0.5 * up * (1.0 - bend * bend) * GELU_C * (
                    1.0 + 3.0 * GELU_K * square
                )
                return carry

            lax.fori_loop(0, ffc // 256, up_tile, 0)
            w_ready(l, 3)
            p = sum_begin()
            product_nt(p, act.at[l], wd.at[l], width)

            def end_norm(c, total):
                value = x2[l, crow(c)] + total + vrow(bias_row(l, 5))
                if l + 1 < layers:
                    x1[crow(c)] = value
                    first_norm(l + 1, crow(c), value)
                else:
                    out_ref[crow(c)] = value.astype(BF16)

            sum_finish(p, end_norm)
            if l + 1 < layers:
                w_forward(l + 1, 0)
                w_ready(l + 1, 0)

        for l in range(layers):
            forward_layer(l)

        g_all = [gq, gw, gu, gd]
        c_all = [cq, co, cu, cd]
        r_all = [rq, ro, ru, rd]

        def c_copy(l, m, q):
            g = q * 2 + 1 - core
            return remote(
                g_all[m].at[prow(g)], c_all[m].at[l, pl.ds(q * piece, piece)],
                csend.at[l, m, q], crecv.at[l, m, q], sibling,
            )

        def h_copy(l, m, t):
            return remote(
                g_all[m].at[prow(chip_to[t])], r_all[m].at[t + 1, l],
                hsend.at[l, m, t], hrecv.at[l, m, t], device_at("flat", chip_to[t]),
            )

        def own_out(l, m):
            return pltpu.make_async_copy(
                g_all[m].at[prow(rank)], r_all[m].at[0, l], own_sem.at[l, m]
            )

        def share_core(l, m):
            for q in range(chips):
                c_copy(l, m, q).start()

        def share_chip(l, m):
            for q in range(chips):
                c_copy(l, m, q).wait_recv()
                mine_rows = prow(q * 2 + core)
                g_all[m][mine_rows] = (
                    g_all[m][mine_rows].astype(F32)
                    + c_all[m][l, q * piece : (q + 1) * piece].astype(F32)
                ).astype(BF16)
            for t in range(chips - 1):
                h_copy(l, m, t).start()
            own_out(l, m).start()

        def share_drain(l, m):
            for q in range(chips):
                c_copy(l, m, q).wait_send()
            for t in range(chips - 1):
                h_copy(l, m, t).wait_send()
            own_out(l, m).wait()

        def share_end(l, m):
            for t in range(chips - 1):
                h_copy(l, m, t).wait_recv()

        def dkv_copy(l, s, d):
            return remote(
                dkv_out.at[d - 1, srow(s)], dkv_in.at[l, d - 1, srow(s)],
                dsend.at[l, d - 1, s], drecv.at[l, d - 1, s],
                device_at("ctx", lax.rem(here + ctx_count - d, ctx_count)),
            )

        def dkv_drain(l):
            for s in range(seqs):
                for d in range(1, back + 1):
                    @pl.when(here - d >= 0)
                    def _():
                        dkv_copy(l, s, d).wait_send()

        def add_term(r, value):
            term[r : r + 1, :] = term[r : r + 1, :] + value

        def backward_layer(l):
            last = l == layers - 1

            def cast(c, carry):
                value = go_ref[crow(c)].astype(F32) if last else gy[crow(c)]
                if last:
                    gy[crow(c)] = value
                gyb[crow(c)] = value.astype(BF16)
                add_term(bias_row(l, 5), colsum(value))
                return carry

            lax.fori_loop(0, chunks, cast, 0)

            def up_back(t, carry):
                off = pl.ds(pl.multiple_of(t * 256, 256), 256)
                dup = nn(gyb[...], wd[l, :, off]) * gs[l, :, off]
                term[pl.ds(bias_row(l, 6) + me, 1), off] = colsum(dup)
                dub[:, off] = dup.astype(BF16)
                return carry

            lax.fori_loop(0, ffc // 256, up_back, 0)
            p = sum_begin()
            product_nt(p, dub, wu.at[l], width)
            if not last:
                share_chip(l + 1, 0)
                share_chip(l + 1, 1)
                share_drain(l + 1, 2)
                share_drain(l + 1, 3)

            def unit_grads(c):
                off = pl.ds(pl.multiple_of(c * LANES, LANES), LANES)
                gd[off] = tn(gyb[:, off], act[l]).astype(BF16)
                gu[off] = tn(a2[l, :, off], dub[...]).astype(BF16)

            def second_back(c, total):
                normed, inverse = norm_parts(x2[l, crow(c)])
                add_term(gain_row(l, 1), colsum(total * normed))
                add_term(bias_row(l, 1), colsum(total))
                value = gy[crow(c)] + norm_back(total, normed, inverse, vrow(gain_row(l, 1)))
                add_term(bias_row(l, 4), colsum(value))
                gy[crow(c)] = value

            sum_finish(p, second_back, unit_grads)
            share_core(l, 2)
            share_core(l, 3)
            gyb[...] = gy[...].astype(BF16)
            dctx[...] = nn(gyb[...], wo[l]).astype(BF16)
            if not last:
                share_drain(l + 1, 0)
                share_drain(l + 1, 1)
                dkv_drain(l + 1)
            for s in range(seqs):
                stacked(qst, qkv[l, srow(s), :cols] * BF16(1.0 / math.sqrt(HEAD)))
                stacked(dst, dctx[srow(s), :])
                product = dctx[srow(s), :].astype(F32) * ctxs[l, srow(s)].astype(F32)
                deltas = [
                    jnp.sum(jnp.where(head_lanes[h], product, 0.0), -1, keepdims=True)
                    for h in range(heads)
                ]
                for d in range(back, -1, -1):
                    keys, values = key_block(l, s, d)
                    score = nt(qst[...], keys)
                    gprob = nt(dst[...], values)
                    mask, dist = block_mask(s, d), block_dist(d)
                    probs, gscores = [], []
                    for h in range(heads):
                        hrow = slice(h * rows, (h + 1) * rows)
                        raw = score[hrow] - slopes[h] * dist - lse[l * seqs + s, hrow, :]
                        prob = jnp.where(mask, jnp.exp(jnp.where(mask, raw, 0.0)), 0.0)
                        probs.append(prob.astype(BF16))
                        gscores.append((prob * (gprob[hrow] - deltas[h])).astype(BF16))
                    probs = jnp.concatenate(probs, 0)
                    gscores = jnp.concatenate(gscores, 0)
                    gkeys = tn(gscores, qst[...])
                    gvalues = tn(probs, dst[...])
                    if d:
                        dkv_out[d - 1, srow(s), :cols] = gkeys.astype(BF16)
                        dkv_out[d - 1, srow(s), cols:] = gvalues.astype(BF16)

                        @pl.when(here - d >= 0)
                        def _():
                            dkv_copy(l, s, d).start()
                    else:
                        dkv0[srow(s), :cols] = gkeys
                        dkv0[srow(s), cols:] = gvalues
                    step = nn(gscores, keys)
                    acc[...] = step if d == back else acc[...] + step
                out = jnp.zeros((rows, cols), F32)
                for h in range(heads):
                    out = jnp.where(head_lanes[h], acc[h * rows : (h + 1) * rows, :], out)
                out = out * (1.0 / math.sqrt(HEAD))
                rq_row = bias_row(l, 2)
                term[rq_row : rq_row + 1, mine] = term[rq_row : rq_row + 1, mine] + colsum(out)
                dqkv[srow(s), :cols] = out.astype(BF16)

            def out_grads(c, carry):
                off = pl.ds(pl.multiple_of(c * LANES, LANES), LANES)
                gw[off] = tn(gyb[:, off], ctxs[l]).astype(BF16)
                return carry

            lax.fori_loop(0, tiles, out_grads, 0)
            for s in range(seqs):
                for d in range(1, back + 1):
                    @pl.when(here + d < ctx_count)
                    def _():
                        dkv_copy(l, s, d).wait_recv()
                        dkv0[srow(s), :] = dkv0[srow(s), :] + dkv_in[l, d - 1, srow(s)].astype(F32)
            rv_row = bias_row(l, 3)
            term[rv_row : rv_row + 1, mine] = colsum(dkv0[:, cols:])
            dqkv[:, cols:] = dkv0[...].astype(BF16)
            p = sum_begin()
            product_nt(p, dqkv, wq.at[l], width)
            share_core(l, 1)
            share_chip(l, 3)
            share_chip(l, 2)

            def in_grads(c):
                off = pl.ds(pl.multiple_of(c * LANES, LANES), LANES)
                gq[off] = tn(a1[l, :, off], dqkv[...]).astype(BF16)

            def first_back(c, total):
                base = x0_ref[crow(c)].astype(F32) if l == 0 else x1[crow(c)]
                normed, inverse = norm_parts(base)
                add_term(gain_row(l, 0), colsum(total * normed))
                add_term(bias_row(l, 0), colsum(total))
                value = gy[crow(c)] + norm_back(total, normed, inverse, vrow(gain_row(l, 0)))
                if l == 0:
                    gin_ref[crow(c)] = value.astype(BF16)
                else:
                    gy[crow(c)] = value

            sum_finish(p, first_back, in_grads)
            share_core(l, 0)

        for l in reversed(range(layers)):
            backward_layer(l)

        alike = [gain_row(l, i) for l in range(layers) for i in range(2)] + [
            bias_row(l, j) for l in range(layers) for j in (0, 1, 4, 5)
        ]

        @pl.when(me != 0)
        def _():
            for r in alike:
                term[r : r + 1, :] = jnp.zeros((1, width), F32)

        def t1_copy(t, g):
            to = lax.rem(rank + t + 1, owners)
            tile = pl.ds(pl.multiple_of((to // group) * LANES, LANES), LANES)
            return remote(term.at[:, tile], tland.at[g], t1send.at[t], t1recv.at[t], plane[t])

        def t2_copy(t):
            return remote(tsum, tz.at[t], t2send.at[t], t2recv.at[t], zpeers[t])

        for t in range(owners - 1):
            t1_copy(t, rank).start()
        share_chip(0, 1)
        share_chip(0, 0)
        own_tile = pl.ds(pl.multiple_of((rank // group) * LANES, LANES), LANES)
        total = term[:, own_tile]
        for t in range(owners - 1):
            source = lax.rem(rank + owners - 1 - t, owners)
            t1_copy(t, source).wait_recv()
            total = total + tland[source]
        tsum[...] = total
        for t in range(mp_count - 1):
            t2_copy(t).start()
        for t in range(mp_count - 1):
            t2_copy(t).wait_recv()
            total = total + tz[t]
        term_out[...] = total

        for m in range(4):
            share_drain(0, m)
            for l in range(layers):
                share_end(l, m)
                for t in range(chips - 1):
                    w_copy(l, m, t, rank).wait_send()
                for t in range(chips):
                    f_copy(l, m, t, rank).wait_send()
        dkv_drain(0)
        sum_drain(0)
        sum_drain(1)
        for t in range(mp_count - 1):
            vz_copy(t).wait_send()
            t2_copy(t).wait_send()
        for t in range(owners - 1):
            v2_copy(t, rank).wait_send()
            t1_copy(t, rank).wait_send()
        for d in range(1, back + 1):
            @pl.when(here + d < ctx_count)
            def _():
                seg_copy(d).wait_send()
                for l in range(layers):
                    for s in range(seqs):
                        kv_copy(l, s, d).wait_send()

    def vm(*shape, dtype=BF16):
        return pltpu.VMEM(shape, dtype)

    def dma(*shape):
        return pltpu.SemaphoreType.DMA(shape)

    scratch = [vm(layers, width, n) for n in sizes]
    scratch += [
        vm(tokens, width, dtype=F32),
        vm(layers, tokens, width, dtype=F32),
        vm(layers, tokens, width),
        vm(layers, tokens, 3 * cols),
        vm(layers, back, tokens, 2 * cols),
        vm(layers, tokens, cols),
        vm(layers * seqs, stack, 1, dtype=F32),
        vm(layers, tokens, width),
        vm(layers, tokens, ffc, dtype=F32),
        vm(layers, tokens, ffc),
    ]
    scratch += [vm(2, tokens, width)] * 5
    scratch += [
        vm(tokens, width, dtype=F32),
        vm(tokens, width),
        vm(tokens, ffc),
        vm(tokens, cols),
        vm(tokens, 3 * cols),
        vm(tokens, 2 * cols, dtype=F32),
        vm(back, tokens, 2 * cols),
        vm(layers, back, tokens, 2 * cols),
    ]
    scratch += [vm(width, n) for n in sizes]
    scratch += [vm(layers, width // 2, n) for n in sizes]
    scratch += [
        vm(mp_count - 1, VEC_ROWS, LANES),
        vm(owners, VEC_ROWS, LANES),
        vm(VEC_ROWS, LANES),
        vm(VEC_ROWS, width, dtype=F32),
        vm(back, 8, rows, dtype=jnp.int32),
        vm(VEC_ROWS, width, dtype=F32),
        vm(owners, VEC_ROWS, LANES, dtype=F32),
        vm(VEC_ROWS, LANES, dtype=F32),
        vm(mp_count - 1, VEC_ROWS, LANES, dtype=F32),
        vm(stack, cols, dtype=F32),
        vm(stack, cols),
        vm(stack, cols),
    ]
    scratch += [
        dma(layers, 4),
        dma(layers, 4, chips - 1), dma(layers, 4, chips - 1),
        dma(layers, 4, chips), dma(layers, 4, chips),
        dma(2, chunks), dma(2, chunks), dma(2, chunks), dma(2, chunks),
        dma(mp_count - 1), dma(mp_count - 1),
        dma(owners - 1), dma(owners - 1),
        dma(layers + 1, back, seqs), dma(layers + 1, back, seqs),
        dma(1), dma(1),
        dma(layers, back, seqs), dma(layers, back, seqs),
        dma(layers, 4, chips), dma(layers, 4, chips),
        dma(layers, 4, chips - 1), dma(layers, 4, chips - 1),
        dma(layers, 4),
        dma(owners - 1), dma(owners - 1),
        dma(mp_count - 1), dma(mp_count - 1),
    ]
    return pl.pallas_call(
        kernel,
        out_shape=[
            jax.ShapeDtypeStruct((tokens, width), BF16),
            jax.ShapeDtypeStruct((tokens, width), BF16),
            jax.ShapeDtypeStruct((VEC_ROWS, LANES), F32),
        ]
        + [jax.ShapeDtypeStruct((chips, layers, piece, n), BF16) for n in sizes],
        in_specs=[VMEM] * 5 + [ANY] * 4,
        out_specs=[VMEM] * 3 + [ANY] * 4,
        scratch_shapes=scratch,
        compiler_params=pltpu.CompilerParams(
            collective_id=0, has_side_effects=True, vmem_limit_bytes=62 * 1024 * 1024
        ),
        name="both_layers",
    )(x0, gout, seg, seg_t, vec, *weights)


def per_device(hidden_in, segment_ids, gains, biases, w_qkv, w_out_t, w_up, w_down_t, grad_out):
    seqs, rows, width = hidden_in.shape
    layers = w_qkv.shape[0]
    cols = w_qkv.shape[3]
    ffc = w_up.shape[2]
    piece = w_qkv.shape[1]
    part = gains.shape[2]
    ctx_count = lax.axis_size("ctx")
    mp_count = lax.axis_size("mp")
    owners = lax.axis_size("batch") * ctx_count
    rank = lax.axis_index("batch") * ctx_count + lax.axis_index("ctx")
    flat = rank * mp_count + lax.axis_index("mp")
    offset = lax.rem(flat * part, LANES)
    vectors = jnp.concatenate([gains.reshape(-1, part), biases.reshape(-1, part)], 0)
    vec_rows = vectors.shape[0]
    vec = lax.dynamic_update_slice(
        jnp.zeros((VEC_ROWS, LANES), BF16), vectors, (0, offset)
    )
    seg = jnp.pad(segment_ids, ((0, 8 - seqs), (0, 0)))
    seg_t = jnp.transpose(segment_ids)
    dims = (layers, seqs, rows, width, cols, ffc, part, owners, ctx_count, mp_count, True)
    output, grad_in, terms, gq, go, gu, gd = run_all(
        hidden_in.reshape(seqs * rows, width),
        grad_out.reshape(seqs * rows, width),
        seg, seg_t, vec,
        [w_qkv.reshape(layers, piece, 3 * cols), w_out_t, w_up, w_down_t],
        dims,
    )
    terms = lax.dynamic_slice(terms, (0, offset), (vec_rows, part))
    split = layers * gains.shape[1]

    def total(slots):
        acc = slots[0].astype(F32)
        for t in range(1, slots.shape[0]):
            acc = acc + slots[t].astype(F32)
        return acc

    return (
        output.reshape(hidden_in.shape),
        grad_in.reshape(hidden_in.shape),
        terms[:split].reshape(gains.shape),
        terms[split:].reshape(biases.shape),
        total(gq).reshape(w_qkv.shape),
        total(go),
        total(gu),
        total(gd),
    )


def solution(mesh):
    in_specs = (
        P("batch", "ctx", None),
        P("batch", "ctx"),
        P(None, None, ("batch", "ctx", "mp")),
        P(None, None, ("batch", "ctx", "mp")),
        P(None, ("batch", "ctx"), None, "mp"),
        P(None, ("batch", "ctx"), "mp"),
        P(None, ("batch", "ctx"), "mp"),
        P(None, ("batch", "ctx"), "mp"),
        P("batch", "ctx", None),
    )
    out_specs = (
        P("batch", "ctx", None),
        P("batch", "ctx", None),
        P(None, None, ("batch", "ctx", "mp")),
        P(None, None, ("batch", "ctx", "mp")),
        P(None, ("batch", "ctx"), None, "mp"),
        P(None, ("batch", "ctx"), "mp"),
        P(None, ("batch", "ctx"), "mp"),
        P(None, ("batch", "ctx"), "mp"),
    )
    return jax.shard_map(
        per_device, mesh=mesh, in_specs=in_specs, out_specs=out_specs, check_vma=False
    )
```

```python
import math

import jax
import jax.numpy as jnp
from jax import lax
from jax.experimental import pallas as pl
from jax.experimental.pallas import tpu as pltpu
from jax.sharding import PartitionSpec as P

HEADS = 16
HEAD = 64
EPS = 1e-05
GELU_C = 0.7978845608028654
GELU_K = 0.044715
LANES = 128
VEC_ROWS = 32
CHUNK = 32
LAG = 2
F32 = jnp.float32
BF16 = jnp.bfloat16

MESH = pl.DeviceIdType.MESH
ANY = pl.BlockSpec(memory_space=pl.ANY)
VMEM = pl.BlockSpec(memory_space=pltpu.VMEM)


def nn(a, b):
    return lax.dot_general(a, b, (((1,), (0,)), ((), ())), preferred_element_type=F32)


def nt(a, b):
    return lax.dot_general(a, b, (((1,), (1,)), ((), ())), preferred_element_type=F32)


def tn(a, b):
    return lax.dot_general(a, b, (((0,), (0,)), ((), ())), preferred_element_type=F32)


def norm_parts(values):
    center = values - jnp.mean(values, -1, keepdims=True)
    inverse = lax.rsqrt(jnp.mean(center * center, -1, keepdims=True) + EPS)
    return center * inverse, inverse


def norm_back(grad_y, normed, inverse, gain):
    scaled = grad_y * gain
    return inverse * (
        scaled
        - jnp.mean(scaled, -1, keepdims=True)
        - normed * jnp.mean(scaled * normed, -1, keepdims=True)
    )


def device_at(kind, rank):
    if kind in ("mp", "ctx"):
        return {kind: rank}
    count = lax.axis_size("ctx")
    return {"batch": rank // count, "ctx": lax.rem(rank, count)}


def remote(src, dst, send, recv, device):
    return pltpu.make_async_remote_copy(
        src_ref=src, dst_ref=dst, send_sem=send, recv_sem=recv,
        device_id=device, device_id_type=MESH,
    )


def colsum(values):
    return jnp.sum(values, 0, keepdims=True)


def run_all(x0, gout, seg, seg_t, vec, weights, dims):
    (layers, seqs, rows, width, cols, ffc, part, owners, ctx_count, mp_count) = dims
    tokens = seqs * rows
    chips = owners // 2
    piece = width // owners
    heads = cols // HEAD
    stack = heads * rows
    back = (ctx_count * rows // 2 + rows - 2) // rows
    chunks = tokens // CHUNK
    sizes = [w.shape[-1] for w in weights]
    tiles = width // LANES
    group = owners // tiles

    def kernel(
        x0_ref, go_ref, seg_ref, segt_ref, vec_ref, wq_in, wo_in, wu_in, wd_in,
        out_ref, gin_ref, term_out, rq, ro, ru, rd,
        wq, wo, wu, wd, x1, x2, a1, qkv, kvl, ctxs, lse, a2, gs, act,
        part_b, out_a, out_b, land_a, land_b, gy, gyb, gxb, dub, dctx, dqkv, dkv0,
        dkv_out, dkv_in, gq, gw, gu, gd, cq, co, cu, cd,
        vz, vland, vsum, vecs, kseg, term, tland, tsum, tz, acc, qst, dst,
        loc_sem, wsend, wrecv, fsend, frecv, asend, arecv, bsend, brecv,
        vsend, vrecv, v2send, v2recv, ksend, krecv, gsend, grecv, dsend, drecv,
        csend, crecv, hsend, hrecv, own_sem, t1send, t1recv, t2send, t2recv,
    ):
        me = lax.axis_index("mp")
        here = lax.axis_index("ctx")
        rank = lax.axis_index("batch") * ctx_count + here
        chip = rank // 2
        core = lax.rem(rank, 2)
        sib_rank = chip * 2 + 1 - core
        sibling = device_at("flat", sib_rank)
        side = device_at("mp", me + 1 - 2 * lax.rem(me, 2))
        across = device_at("mp", mp_count - 1 - me)
        is_mid = (me == 1) | (me == 2)
        is_end = (me == 0) | (me == 3)
        zpeers = [device_at("mp", lax.rem(me + t, mp_count)) for t in range(1, mp_count)]
        plane = [device_at("flat", lax.rem(rank + t, owners)) for t in range(1, owners)]
        chip_to = [lax.rem(chip + t, chips) * 2 + core for t in range(1, chips)]
        chip_from = [lax.rem(chip + chips - t, chips) * 2 + core for t in range(1, chips)]
        w_in = [wq_in, wo_in, wu_in, wd_in]
        w_all = [wq, wo, wu, wd]

        def prow(g):
            return pl.ds(pl.multiple_of(g * piece, piece), piece)

        def crow(c):
            return pl.ds(pl.multiple_of(c * CHUNK, CHUNK), CHUNK)

        def srow(s):
            return pl.ds(s * rows, rows)

        def w_rows(l, m, g):
            return w_all[m].at[l, :, prow(g)] if m == 0 else w_all[m].at[l, prow(g)]

        def own_copy(l, m):
            return pltpu.make_async_copy(
                w_in[m].at[l], w_rows(l, m, rank), loc_sem.at[l, m]
            )

        def w_copy(l, m, t, g):
            return remote(
                w_in[m].at[l], w_rows(l, m, g),
                wsend.at[l, m, t], wrecv.at[l, m, t], device_at("flat", chip_to[t]),
            )

        def f_copy(l, m, t, g):
            src = w_in[m].at[l] if t == 0 else w_rows(l, m, g)
            return remote(
                src, w_rows(l, m, g), fsend.at[l, m, t], frecv.at[l, m, t], sibling
            )

        def w_issue(l, m):
            for t in range(chips - 1):
                w_copy(l, m, t, rank).start()
            f_copy(l, m, 0, rank).start()
            own_copy(l, m).start()

        def w_forward(l, m):
            for t in range(chips - 1):
                w_copy(l, m, t, chip_from[t]).wait_recv()
                f_copy(l, m, t + 1, chip_from[t]).start()

        def w_ready(l, m):
            own_copy(l, m).wait()
            f_copy(l, m, 0, sib_rank).wait_recv()
            for t in range(chips - 1):
                f_copy(l, m, t + 1, chip_from[t] + 1 - 2 * core).wait_recv()

        barrier = pltpu.get_barrier_semaphore()
        for device in zpeers + plane:
            pl.semaphore_signal(barrier, inc=1, device_id=device, device_id_type=MESH)
        pl.semaphore_wait(barrier, len(zpeers) + len(plane))

        def vz_copy(t):
            return remote(vec_ref, vz.at[t], vsend.at[t], vrecv.at[t], zpeers[t])

        for t in range(mp_count - 1):
            vz_copy(t).start()
        w_issue(0, 0)
        w_issue(0, 1)
        w_issue(0, 2)

        def seg_copy(d):
            return remote(
                seg_ref, kseg.at[d - 1], ksend.at[layers, d - 1, 0], krecv.at[layers, d - 1, 0],
                device_at("ctx", lax.rem(here + d, ctx_count)),
            )

        for d in range(1, back + 1):
            @pl.when(here + d < ctx_count)
            def _():
                seg_copy(d).start()

            @pl.when(here - d < 0)
            def _():
                kseg[d - 1] = jnp.full(kseg.shape[1:], -1, jnp.int32)
                for l in range(layers):
                    kvl[l, d - 1] = jnp.zeros(kvl.shape[2:], BF16)

        vtot = vec_ref[...].astype(F32)
        for t in range(mp_count - 1):
            vz_copy(t).wait_recv()
            vtot = vtot + vz[t].astype(F32)
        vsum[...] = vtot.astype(BF16)

        def v2_copy(t, g):
            return remote(vsum, vland.at[g], v2send.at[t], v2recv.at[t], plane[t])

        for t in range(owners - 1):
            v2_copy(t, rank).start()
        vland[rank] = vsum[...]
        for t in range(owners - 1):
            v2_copy(t, lax.rem(rank + owners - 1 - t, owners)).wait_recv()
        for t in range(tiles):
            tile = vland[t * group].astype(F32)
            for j in range(1, group):
                tile = tile + vland[t * group + j].astype(F32)
            vecs[:, t * LANES : (t + 1) * LANES] = tile
        term[...] = jnp.zeros(term.shape, F32)
        for d in range(1, back + 1):
            @pl.when(here - d >= 0)
            def _():
                seg_copy(d).wait_recv()

        mine = pl.ds(pl.multiple_of(me * cols, LANES), cols)

        def gain_row(l, i):
            return l * 2 + i

        def bias_row(l, j):
            return layers * 2 + l * 10 + j

        def vrow(r):
            return vecs[r : r + 1, :]

        lane_head = lax.broadcasted_iota(jnp.int32, (rows, cols), 1) // HEAD
        head_lanes = [lane_head == h for h in range(heads)]
        row_i = lax.broadcasted_iota(jnp.int32, (rows, rows), 0)
        col_j = lax.broadcasted_iota(jnp.int32, (rows, rows), 1)
        slopes = [
            jnp.exp2(
                jnp.full((1, rows), -8.0 / HEADS, F32)
                * (me * heads + (h + 1)).astype(F32)
            )
            for h in range(heads)
        ]

        def stacked(ref, values):
            for h in range(heads):
                ref[h * rows : (h + 1) * rows, :] = jnp.where(
                    head_lanes[h], values, jnp.zeros_like(values)
                )

        def block_mask(s, d):
            keys = (seg_ref if d == 0 else kseg.at[d - 1])[s : s + 1, :]
            mask = segt_ref[:, s : s + 1] == keys
            return mask & (col_j <= row_i) if d == 0 else mask

        def block_dist(d):
            return (d * rows + row_i - col_j).astype(F32)

        def key_block(l, s, d):
            if d == 0:
                return qkv[l, srow(s), cols : 2 * cols], qkv[l, srow(s), 2 * cols : 3 * cols]
            return kvl[l, d - 1, srow(s), :cols], kvl[l, d - 1, srow(s), cols:]

        def side_copy(p, c, src):
            return remote(
                src.at[p, crow(c)], land_a.at[p, crow(c)], asend.at[p, c], arecv.at[p, c], side
            )

        def cross_copy(p, c):
            return remote(
                out_b.at[p, crow(c)], land_b.at[p, crow(c)], bsend.at[p, c], brecv.at[p, c], across
            )

        per_seq = rows // CHUNK

        def sum_drain(p, low, high):
            def body(c, carry):
                side_copy(p, c, part_b).wait_send()

                @pl.when(is_mid)
                def _():
                    cross_copy(p, c).wait_send()

                return carry

            lax.fori_loop(low, high, body, 0)

        begun = [0] * seqs

        def sum_begin(s):
            k = begun[s]
            begun[s] += 1
            if k >= 2:
                sum_drain(k % 2, s * per_seq, (s + 1) * per_seq)
            return k % 2

        def sum_start(p, s):
            @pl.when(is_end)
            def _():
                for c in range(s * per_seq, (s + 1) * per_seq):
                    side_copy(p, c, part_b).start()

        def sum_plan(p, consumer):
            def pair_up(c):
                @pl.when(is_mid)
                def _():
                    side_copy(p, c, part_b).wait_recv()
                    pair = part_b[p, crow(c)].astype(F32) + land_a[p, crow(c)].astype(F32)
                    out_b[p, crow(c)] = pair.astype(BF16)
                    cross_copy(p, c).start()

            def close(c):
                @pl.when(is_mid)
                def _():
                    cross_copy(p, c).wait_recv()
                    total = out_b[p, crow(c)].astype(F32) + land_b[p, crow(c)].astype(F32)
                    out_a[p, crow(c)] = total.astype(BF16)
                    side_copy(p, c, out_a).start()

            def use(c):
                @pl.when(is_end)
                def _():
                    side_copy(p, c, part_b).wait_recv()
                    out_a[p, crow(c)] = land_a[p, crow(c)]

                consumer(c, out_a[p, crow(c)].astype(F32))

            pairs = [lambda c=c: pair_up(c) for c in range(chunks)]
            closes = [lambda c=c: close(c) for c in range(chunks)]
            uses = [lambda c=c: use(c) for c in range(chunks)]
            early, wait, host = pairs[:LAG], [], []
            for c in range(per_seq):
                wait += [pairs[c + LAG], closes[c], uses[c]]
            for c in range(per_seq, chunks - 1):
                host += pairs[c + LAG : c + LAG + 1] + [closes[c]]
            return early, wait, host, [closes[-1]] + uses[per_seq:]

        def weave(main, side_steps, lead=0):
            for i, step in enumerate(main):
                step()
                if i >= lead and side_steps:
                    side_steps.pop(0)()

        def finish(side_steps, fillers=(), share=1):
            while side_steps:
                for _ in range(share):
                    if fillers:
                        fillers.pop(0)()
                side_steps.pop(0)()

        def run_steps(fillers):
            while fillers:
                fillers.pop(0)()

        def product_steps(p, s, left, weight):
            def tile(t):
                off = slice(t * 256, (t + 1) * 256)
                part_b[p, srow(s), off] = nt(left(), weight(off)).astype(BF16)

            return [lambda t=t: tile(t) for t in range(width // 256)]

        def kv_copy(l, s, d):
            return remote(
                qkv.at[l, srow(s), pl.ds(cols, 2 * cols)], kvl.at[l, d - 1, srow(s)],
                ksend.at[l, d - 1, s], krecv.at[l, d - 1, s],
                device_at("ctx", lax.rem(here + d, ctx_count)),
            )

        def first_norm(l, rws, x):
            normed, _ = norm_parts(x)
            a1[l, rws] = (normed * vrow(gain_row(l, 0)) + vrow(bias_row(l, 0))).astype(BF16)

        def start_norm(c, carry):
            first_norm(0, crow(c), x0_ref[crow(c)].astype(F32))
            return carry

        lax.fori_loop(0, tokens // CHUNK, start_norm, 0)
        w_forward(0, 0)
        w_issue(0, 3)
        w_ready(0, 0)
        scale = 1.0 / math.sqrt(HEAD)

        def qkv_steps(l, s):
            def kind(u):
                value = nn(a1[l, srow(s)], wq[l, u])
                if u != 1:
                    r = bias_row(l, 2 if u == 0 else 3)
                    value = value + vecs[r : r + 1, mine]
                qkv[l, srow(s), u * cols : (u + 1) * cols] = value.astype(BF16)
                if u == 2:
                    for d in range(1, back + 1):
                        @pl.when(here + d < ctx_count)
                        def _():
                            kv_copy(l, s, d).start()

            return [lambda u=u: kind(u) for u in (1, 2, 0)]

        def attend_steps(l, s):
            totals = [jnp.zeros((rows, 1), F32)] * heads

            def block(d):
                if d == 0:
                    stacked(qst, qkv[l, srow(s), :cols] * BF16(scale))
                else:
                    @pl.when(here - d >= 0)
                    def _():
                        kv_copy(l, s, d).wait_recv()
                keys, values = key_block(l, s, d)
                score = nt(qst[...], keys)
                mask, dist = block_mask(s, d), block_dist(d)
                expos = []
                for h in range(heads):
                    raw = score[h * rows : (h + 1) * rows] - slopes[h] * dist
                    expo = jnp.where(mask, jnp.exp(jnp.where(mask, raw, 0.0)), 0.0)
                    totals[h] = totals[h] + jnp.sum(expo, -1, keepdims=True)
                    expos.append(expo.astype(BF16))
                step = nn(jnp.concatenate(expos, 0), values)
                acc[...] = step if d == 0 else acc[...] + step

            def close():
                out = jnp.zeros((rows, cols), F32)
                for h in range(heads):
                    lse[l * seqs + s, h * rows : (h + 1) * rows, :] = jnp.log(totals[h])
                    out = jnp.where(head_lanes[h], acc[h * rows : (h + 1) * rows, :] / totals[h], out)
                ctxs[l, srow(s)] = out.astype(BF16)

            return [lambda d=d: block(d) for d in range(back + 1)] + [close]

        def mid_norm(l):
            def consumer(c, total):
                base = x0_ref[crow(c)].astype(F32) if l == 0 else x1[crow(c)]
                value = base + total + vrow(bias_row(l, 4))
                x2[l, crow(c)] = value
                normed, _ = norm_parts(value)
                a2[l, crow(c)] = (
                    normed * vrow(gain_row(l, 1)) + vrow(bias_row(l, 1))
                ).astype(BF16)

            return consumer

        def end_norm(l):
            def consumer(c, total):
                value = x2[l, crow(c)] + total + vrow(bias_row(l, 5))
                if l + 1 < layers:
                    x1[crow(c)] = value
                    first_norm(l + 1, crow(c), value)
                else:
                    out_ref[crow(c)] = value.astype(BF16)

            return consumer

        def up_steps(l, s):
            def tile(t):
                off = slice(t * 256, (t + 1) * 256)
                up = nn(a2[l, srow(s)], wu[l, :, off]) + vecs[pl.ds(bias_row(l, 6) + me, 1), off]
                square = up * up
                bend = jnp.tanh(GELU_C * (up + GELU_K * square * up))
                half = 0.5 * (1.0 + bend)
                act[l, srow(s), off] = (up * half).astype(BF16)
                gs[l, srow(s), off] = half + 0.5 * up * (1.0 - bend * bend) * GELU_C * (
                    1.0 + 3.0 * GELU_K * square
                )

            return [lambda t=t: tile(t) for t in range(ffc // 256)]

        first, second = 0, 1

        def forward_layer(l, before):
            host, late = before
            weave(qkv_steps(l, first), host)
            finish(host)
            finish(late)
            weave(qkv_steps(l, second), [])
            w_forward(l, 1)
            if l + 1 < layers:
                w_issue(l + 1, 0)
            p = sum_begin(first)
            steps = attend_steps(l, first) + [lambda: w_ready(l, 1)]
            steps += product_steps(p, first, lambda: ctxs[l, srow(first)], lambda off: wo[l, off, :])
            weave(steps, [])
            sum_start(p, first)
            early, wait, host, late = sum_plan(p, mid_norm(l))
            sum_begin(second)
            steps = attend_steps(l, second)
            steps += product_steps(
                p, second, lambda: ctxs[l, srow(second)], lambda off: wo[l, off, :]
            )
            weave(steps, early, len(steps) - 3)
            sum_start(p, second)
            finish(early)
            w_forward(l, 2)
            if l + 1 < layers:
                w_issue(l + 1, 1)
                w_issue(l + 1, 2)
            finish(wait)
            w_ready(l, 2)
            p = sum_begin(first)
            steps = up_steps(l, first) + [lambda: w_forward(l, 3), lambda: w_ready(l, 3)]
            steps += product_steps(p, first, lambda: act[l, srow(first)], lambda off: wd[l, off, :])
            weave(steps, host, 2)
            sum_start(p, first)
            finish(host)
            finish(late)
            if l + 1 < layers:
                w_issue(l + 1, 3)
            early, wait, host, late = sum_plan(p, end_norm(l))
            sum_begin(second)
            steps = up_steps(l, second)
            steps += product_steps(p, second, lambda: act[l, srow(second)], lambda off: wd[l, off, :])
            weave(steps, early, len(steps) - 3)
            sum_start(p, second)
            if l + 1 < layers:
                finish(early)
                finish(wait)
                w_forward(l + 1, 0)
                w_ready(l + 1, 0)
                return host, late
            return early + wait + host + late, []

        carried = ([], [])
        for l in range(layers):
            carried = forward_layer(l, carried)

        g_all = [gq, gw, gu, gd]
        c_all = [cq, co, cu, cd]
        r_all = [rq, ro, ru, rd]

        def at_rows(m, rws):
            return (slice(None), rws) if m == 0 else (rws,)

        def c_copy(l, m, q):
            g = q * 2 + 1 - core
            return remote(
                g_all[m].at[at_rows(m, prow(g))],
                c_all[m].at[(l,) + at_rows(m, pl.ds(q * piece, piece))],
                csend.at[l, m, q], crecv.at[l, m, q], sibling,
            )

        def h_copy(l, m, t):
            return remote(
                g_all[m].at[at_rows(m, prow(chip_to[t]))], r_all[m].at[t + 1, l],
                hsend.at[l, m, t], hrecv.at[l, m, t], device_at("flat", chip_to[t]),
            )

        def own_out(l, m):
            return pltpu.make_async_copy(
                g_all[m].at[at_rows(m, prow(rank))], r_all[m].at[0, l], own_sem.at[l, m]
            )

        def share_core(l, m):
            for q in range(chips):
                c_copy(l, m, q).start()

        def share_chip_steps(l, m):
            def add(q):
                c_copy(l, m, q).wait_recv()
                at = at_rows(m, prow(q * 2 + core))
                landed = c_all[m][(l,) + at_rows(m, pl.ds(q * piece, piece))]
                g_all[m][at] = (g_all[m][at].astype(F32) + landed.astype(F32)).astype(BF16)

            def send():
                for t in range(chips - 1):
                    h_copy(l, m, t).start()
                own_out(l, m).start()

            return [lambda q=q: add(q) for q in range(chips)] + [send]

        def share_drain(l, m):
            for q in range(chips):
                c_copy(l, m, q).wait_send()
            for t in range(chips - 1):
                h_copy(l, m, t).wait_send()
            own_out(l, m).wait()

        def share_end(l, m):
            for t in range(chips - 1):
                h_copy(l, m, t).wait_recv()

        def dkv_copy(l, s, d):
            return remote(
                dkv_out.at[d - 1, srow(s)], dkv_in.at[l, d - 1, srow(s)],
                dsend.at[l, d - 1, s], drecv.at[l, d - 1, s],
                device_at("ctx", lax.rem(here + ctx_count - d, ctx_count)),
            )

        def dkv_drain(l):
            for s in range(seqs):
                for d in range(1, back + 1):
                    @pl.when(here - d >= 0)
                    def _():
                        dkv_copy(l, s, d).wait_send()

        def add_term(r, value):
            term[r : r + 1, :] = term[r : r + 1, :] + value

        def unit_steps(l, s):
            last = l == layers - 1

            def cast():
                value = go_ref[srow(s)].astype(F32) if last else gy[srow(s)]
                if last:
                    gy[srow(s)] = value
                gyb[srow(s)] = value.astype(BF16)
                add_term(bias_row(l, 5), colsum(value))

            def tile(t):
                off = slice(t * 256, (t + 1) * 256)
                dup = nn(gyb[srow(s)], wd[l, :, off]) * gs[l, srow(s), off]
                row = pl.ds(bias_row(l, 6) + me, 1)
                term[row, off] = term[row, off] + colsum(dup)
                dub[srow(s), off] = dup.astype(BF16)

            return [cast] + [lambda t=t: tile(t) for t in range(ffc // 256)]

        def second_back(l):
            def consumer(c, total):
                normed, inverse = norm_parts(x2[l, crow(c)])
                add_term(gain_row(l, 1), colsum(total * normed))
                add_term(bias_row(l, 1), colsum(total))
                value = gy[crow(c)] + norm_back(total, normed, inverse, vrow(gain_row(l, 1)))
                add_term(bias_row(l, 4), colsum(value))
                gy[crow(c)] = value
                gxb[crow(c)] = value.astype(BF16)

            return consumer

        def first_back(l):
            def consumer(c, total):
                base = x0_ref[crow(c)].astype(F32) if l == 0 else x1[crow(c)]
                normed, inverse = norm_parts(base)
                add_term(gain_row(l, 0), colsum(total * normed))
                add_term(bias_row(l, 0), colsum(total))
                value = gy[crow(c)] + norm_back(total, normed, inverse, vrow(gain_row(l, 0)))
                if l == 0:
                    gin_ref[crow(c)] = value.astype(BF16)
                else:
                    gy[crow(c)] = value

            return consumer

        def attend_back_steps(l, s):
            deltas = []

            def begin():
                dctx[srow(s)] = nn(gxb[srow(s)], wo[l]).astype(BF16)
                stacked(qst, qkv[l, srow(s), :cols] * BF16(scale))
                stacked(dst, dctx[srow(s), :])
                product = dctx[srow(s), :].astype(F32) * ctxs[l, srow(s)].astype(F32)
                for h in range(heads):
                    deltas.append(
                        jnp.sum(jnp.where(head_lanes[h], product, 0.0), -1, keepdims=True)
                    )

            def block(d):
                keys, values = key_block(l, s, d)
                score = nt(qst[...], keys)
                gprob = nt(dst[...], values)
                mask, dist = block_mask(s, d), block_dist(d)
                probs, gscores = [], []
                for h in range(heads):
                    hrow = slice(h * rows, (h + 1) * rows)
                    raw = score[hrow] - slopes[h] * dist - lse[l * seqs + s, hrow, :]
                    prob = jnp.where(mask, jnp.exp(jnp.where(mask, raw, 0.0)), 0.0)
                    probs.append(prob.astype(BF16))
                    gscores.append((prob * (gprob[hrow] - deltas[h])).astype(BF16))
                probs = jnp.concatenate(probs, 0)
                gscores = jnp.concatenate(gscores, 0)
                gkeys = tn(gscores, qst[...])
                gvalues = tn(probs, dst[...])
                if d:
                    dkv_out[d - 1, srow(s), :cols] = gkeys.astype(BF16)
                    dkv_out[d - 1, srow(s), cols:] = gvalues.astype(BF16)

                    @pl.when(here - d >= 0)
                    def _():
                        dkv_copy(l, s, d).start()
                else:
                    dkv0[srow(s), :cols] = gkeys
                    dkv0[srow(s), cols:] = gvalues
                step = nn(gscores, keys)
                acc[...] = step if d == back else acc[...] + step

            def close():
                out = jnp.zeros((rows, cols), F32)
                for h in range(heads):
                    out = jnp.where(head_lanes[h], acc[h * rows : (h + 1) * rows, :], out)
                out = out * scale
                r = bias_row(l, 2)
                term[r : r + 1, mine] = term[r : r + 1, mine] + colsum(out)
                dqkv[srow(s), :cols] = out.astype(BF16)

            return [begin] + [lambda d=d: block(d) for d in range(back, -1, -1)] + [close]

        def gather_dkv(l, s):
            for d in range(back, 0, -1):
                @pl.when(here + d < ctx_count)
                def _():
                    dkv_copy(l, s, d).wait_recv()
                    dkv0[srow(s), :] = dkv0[srow(s), :] + dkv_in[l, d - 1, srow(s)].astype(F32)
            r = bias_row(l, 3)
            term[r : r + 1, mine] = term[r : r + 1, mine] + colsum(dkv0[srow(s), cols:])
            dqkv[srow(s), cols:] = dkv0[srow(s), :].astype(BF16)

        def in_product_steps(p, l, s):
            def tile(t):
                off = slice(t * 256, (t + 1) * 256)
                value = nt(dqkv[srow(s), :cols], wq[l, 0, off, :])
                for u in (1, 2):
                    value = value + nt(dqkv[srow(s), u * cols : (u + 1) * cols], wq[l, u, off, :])
                part_b[p, srow(s), off] = value.astype(BF16)

            return [lambda t=t: tile(t) for t in range(width // 256)]

        def grad_tiles(one):
            return [lambda c=c: one(slice(c * LANES, (c + 1) * LANES)) for c in range(tiles)]

        def backward_layer(l, before):
            last = l == layers - 1

            def down_grads(off):
                gd[off] = tn(gyb[:, off], act[l]).astype(BF16)

            def up_grads(off):
                gu[off] = tn(a2[l, :, off], dub[...]).astype(BF16)

            def out_grads(off):
                gw[off] = tn(gxb[:, off], ctxs[l]).astype(BF16)

            def in_grads(off):
                for u in range(3):
                    gq[u, off] = tn(
                        a1[l, :, off], dqkv[:, u * cols : (u + 1) * cols]
                    ).astype(BF16)

            host, late = before
            p = sum_begin(first)
            steps = unit_steps(l, first)
            steps += product_steps(p, first, lambda: dub[srow(first)], lambda off: wu[l, off, :])
            weave(steps, host, 3 if last else 1)
            sum_start(p, first)
            finish(host)
            finish(late)
            early, wait, host, late = sum_plan(p, second_back(l))
            sum_begin(second)
            steps = unit_steps(l, second)
            steps += product_steps(p, second, lambda: dub[srow(second)], lambda off: wu[l, off, :])
            weave(steps, early, len(steps) - 3)
            sum_start(p, second)
            finish(early)
            fillers = []
            if not last:
                share_drain(l + 1, 2)
                share_drain(l + 1, 3)
                fillers += share_chip_steps(l + 1, 0) + share_chip_steps(l + 1, 1)
            fillers += grad_tiles(down_grads) + [lambda: share_core(l, 3)]
            fillers += grad_tiles(up_grads) + [lambda: share_core(l, 2)]
            finish(wait, fillers)
            if not last:
                dkv_drain(l + 1)
            weave(attend_back_steps(l, first), host)
            finish(host, fillers)
            finish(late, fillers)
            run_steps(fillers)
            steps = attend_back_steps(l, second)
            steps[-2:] = share_chip_steps(l, 3) + steps[-2:] + share_chip_steps(l, 2)
            run_steps(steps)
            if not last:
                share_drain(l + 1, 0)
                share_drain(l + 1, 1)
            gather_dkv(l, first)
            p = sum_begin(first)
            run_steps(in_product_steps(p, l, first))
            sum_start(p, first)
            early, wait, host, late = sum_plan(p, first_back(l))
            gather_dkv(l, second)
            sum_begin(second)
            steps = in_product_steps(p, l, second)
            weave(steps, early, len(steps) - 2)
            sum_start(p, second)
            finish(early)
            fillers = grad_tiles(out_grads) + [lambda: share_core(l, 1)]
            fillers += grad_tiles(in_grads) + [lambda: share_core(l, 0)]
            finish(wait, fillers, 2)
            run_steps(fillers)
            if l:
                return host, late
            fillers = share_chip_steps(0, 1) + share_chip_steps(0, 0)
            finish(host, fillers)
            finish(late, fillers)
            run_steps(fillers)

        for l in reversed(range(layers)):
            carried = backward_layer(l, carried)

        alike = [gain_row(l, i) for l in range(layers) for i in range(2)] + [
            bias_row(l, j) for l in range(layers) for j in (0, 1, 4, 5)
        ]

        @pl.when(me != 0)
        def _():
            for r in alike:
                term[r : r + 1, :] = jnp.zeros((1, width), F32)

        def t1_copy(t, g):
            to = lax.rem(rank + t + 1, owners)
            tile = pl.ds(pl.multiple_of((to // group) * LANES, LANES), LANES)
            return remote(term.at[:, tile], tland.at[g], t1send.at[t], t1recv.at[t], plane[t])

        def t2_copy(t):
            return remote(tsum, tz.at[t], t2send.at[t], t2recv.at[t], zpeers[t])

        for t in range(owners - 1):
            t1_copy(t, rank).start()
        own_tile = pl.ds(pl.multiple_of((rank // group) * LANES, LANES), LANES)
        total = term[:, own_tile]
        for t in range(owners - 1):
            source = lax.rem(rank + owners - 1 - t, owners)
            t1_copy(t, source).wait_recv()
            total = total + tland[source]
        tsum[...] = total
        for t in range(mp_count - 1):
            t2_copy(t).start()
        for t in range(mp_count - 1):
            t2_copy(t).wait_recv()
            total = total + tz[t]
        term_out[...] = total

        for m in range(4):
            share_drain(0, m)
            for l in range(layers):
                share_end(l, m)
                for t in range(chips - 1):
                    w_copy(l, m, t, rank).wait_send()
                for t in range(chips):
                    f_copy(l, m, t, rank).wait_send()
        dkv_drain(0)
        sum_drain(0, 0, tokens // CHUNK)
        sum_drain(1, 0, tokens // CHUNK)
        for t in range(mp_count - 1):
            vz_copy(t).wait_send()
            t2_copy(t).wait_send()
        for t in range(owners - 1):
            v2_copy(t, rank).wait_send()
            t1_copy(t, rank).wait_send()
        for d in range(1, back + 1):
            @pl.when(here + d < ctx_count)
            def _():
                seg_copy(d).wait_send()
                for l in range(layers):
                    for s in range(seqs):
                        kv_copy(l, s, d).wait_send()

    def vm(*shape, dtype=BF16):
        return pltpu.VMEM(shape, dtype)

    def dma(*shape):
        return pltpu.SemaphoreType.DMA(shape)

    scratch = [vm(layers, 3, width, cols)] + [vm(layers, width, n) for n in sizes[1:]]
    scratch += [
        vm(tokens, width, dtype=F32),
        vm(layers, tokens, width, dtype=F32),
        vm(layers, tokens, width),
        vm(layers, tokens, 3 * cols),
        vm(layers, back, tokens, 2 * cols),
        vm(layers, tokens, cols),
        vm(layers * seqs, stack, 1, dtype=F32),
        vm(layers, tokens, width),
        vm(layers, tokens, ffc, dtype=F32),
        vm(layers, tokens, ffc),
    ]
    scratch += [vm(2, tokens, width)] * 5
    scratch += [
        vm(tokens, width, dtype=F32),
        vm(tokens, width),
        vm(tokens, width),
        vm(tokens, ffc),
        vm(tokens, cols),
        vm(tokens, 3 * cols),
        vm(tokens, 2 * cols, dtype=F32),
        vm(back, tokens, 2 * cols),
        vm(layers, back, tokens, 2 * cols),
    ]
    scratch += [vm(3, width, cols)] + [vm(width, n) for n in sizes[1:]]
    scratch += [vm(layers, 3, width // 2, cols)]
    scratch += [vm(layers, width // 2, n) for n in sizes[1:]]
    scratch += [
        vm(mp_count - 1, VEC_ROWS, LANES),
        vm(owners, VEC_ROWS, LANES),
        vm(VEC_ROWS, LANES),
        vm(VEC_ROWS, width, dtype=F32),
        vm(back, 8, rows, dtype=jnp.int32),
        vm(VEC_ROWS, width, dtype=F32),
        vm(owners, VEC_ROWS, LANES, dtype=F32),
        vm(VEC_ROWS, LANES, dtype=F32),
        vm(mp_count - 1, VEC_ROWS, LANES, dtype=F32),
        vm(stack, cols, dtype=F32),
        vm(stack, cols),
        vm(stack, cols),
    ]
    scratch += [
        dma(layers, 4),
        dma(layers, 4, chips - 1), dma(layers, 4, chips - 1),
        dma(layers, 4, chips), dma(layers, 4, chips),
        dma(2, chunks), dma(2, chunks), dma(2, chunks), dma(2, chunks),
        dma(mp_count - 1), dma(mp_count - 1),
        dma(owners - 1), dma(owners - 1),
        dma(layers + 1, back, seqs), dma(layers + 1, back, seqs),
        dma(1), dma(1),
        dma(layers, back, seqs), dma(layers, back, seqs),
        dma(layers, 4, chips), dma(layers, 4, chips),
        dma(layers, 4, chips - 1), dma(layers, 4, chips - 1),
        dma(layers, 4),
        dma(owners - 1), dma(owners - 1),
        dma(mp_count - 1), dma(mp_count - 1),
    ]
    return pl.pallas_call(
        kernel,
        out_shape=[
            jax.ShapeDtypeStruct((tokens, width), BF16),
            jax.ShapeDtypeStruct((tokens, width), BF16),
            jax.ShapeDtypeStruct((VEC_ROWS, LANES), F32),
        ]
        + [jax.ShapeDtypeStruct((chips,) + w.shape, BF16) for w in weights],
        in_specs=[VMEM] * 5 + [ANY] * 4,
        out_specs=[VMEM] * 3 + [ANY] * 4,
        scratch_shapes=scratch,
        compiler_params=pltpu.CompilerParams(
            collective_id=0, has_side_effects=True, vmem_limit_bytes=62 * 1024 * 1024
        ),
        name="both_layers",
    )(x0, gout, seg, seg_t, vec, *weights)


def per_device(hidden_in, segment_ids, gains, biases, w_qkv, w_out_t, w_up, w_down_t, grad_out):
    seqs, rows, width = hidden_in.shape
    layers = w_qkv.shape[0]
    cols = w_qkv.shape[3]
    ffc = w_up.shape[2]
    piece = w_qkv.shape[1]
    part = gains.shape[2]
    ctx_count = lax.axis_size("ctx")
    mp_count = lax.axis_size("mp")
    owners = lax.axis_size("batch") * ctx_count
    rank = lax.axis_index("batch") * ctx_count + lax.axis_index("ctx")
    flat = rank * mp_count + lax.axis_index("mp")
    offset = lax.rem(flat * part, LANES)
    vectors = jnp.concatenate([gains.reshape(-1, part), biases.reshape(-1, part)], 0)
    vec_rows = vectors.shape[0]
    vec = lax.dynamic_update_slice(
        jnp.zeros((VEC_ROWS, LANES), BF16), vectors, (0, offset)
    )
    seg = jnp.pad(segment_ids, ((0, 8 - seqs), (0, 0)))
    seg_t = jnp.transpose(segment_ids)
    dims = (layers, seqs, rows, width, cols, ffc, part, owners, ctx_count, mp_count)
    output, grad_in, terms, gq, go, gu, gd = run_all(
        hidden_in.reshape(seqs * rows, width),
        grad_out.reshape(seqs * rows, width),
        seg, seg_t, vec,
        [jnp.transpose(w_qkv, (0, 2, 1, 3)), w_out_t, w_up, w_down_t],
        dims,
    )
    terms = lax.dynamic_slice(terms, (0, offset), (vec_rows, part))
    split = layers * gains.shape[1]

    def total(slots):
        acc = slots[0].astype(F32)
        for t in range(1, slots.shape[0]):
            acc = acc + slots[t].astype(F32)
        return acc

    return (
        output.reshape(hidden_in.shape),
        grad_in.reshape(hidden_in.shape),
        terms[:split].reshape(gains.shape),
        terms[split:].reshape(biases.shape),
        jnp.transpose(total(gq), (0, 2, 1, 3)),
        total(go),
        total(gu),
        total(gd),
    )


def solution(mesh):
    in_specs = (
        P("batch", "ctx", None),
        P("batch", "ctx"),
        P(None, None, ("batch", "ctx", "mp")),
        P(None, None, ("batch", "ctx", "mp")),
        P(None, ("batch", "ctx"), None, "mp"),
        P(None, ("batch", "ctx"), "mp"),
        P(None, ("batch", "ctx"), "mp"),
        P(None, ("batch", "ctx"), "mp"),
        P("batch", "ctx", None),
    )
    out_specs = (
        P("batch", "ctx", None),
        P("batch", "ctx", None),
        P(None, None, ("batch", "ctx", "mp")),
        P(None, None, ("batch", "ctx", "mp")),
        P(None, ("batch", "ctx"), None, "mp"),
        P(None, ("batch", "ctx"), "mp"),
        P(None, ("batch", "ctx"), "mp"),
        P(None, ("batch", "ctx"), "mp"),
    )
    return jax.shard_map(
        per_device, mesh=mesh, in_specs=in_specs, out_specs=out_specs, check_vma=False
    )
```

```python
import math

import jax
import jax.numpy as jnp
from jax import lax
from jax.experimental import pallas as pl
from jax.experimental.pallas import tpu as pltpu
from jax.sharding import PartitionSpec as P

HEADS = 16
HEAD = 64
EPS = 1e-05
GELU_C = 0.7978845608028654
GELU_K = 0.044715
LANES = 128
VEC_ROWS = 32
CHUNK = 32
LAG = 2
F32 = jnp.float32
BF16 = jnp.bfloat16

MESH = pl.DeviceIdType.MESH
ANY = pl.BlockSpec(memory_space=pl.ANY)
VMEM = pl.BlockSpec(memory_space=pltpu.VMEM)


def nn(a, b):
    return lax.dot_general(a, b, (((1,), (0,)), ((), ())), preferred_element_type=F32)


def nt(a, b):
    return lax.dot_general(a, b, (((1,), (1,)), ((), ())), preferred_element_type=F32)


def tn(a, b):
    return lax.dot_general(a, b, (((0,), (0,)), ((), ())), preferred_element_type=F32)


def norm_parts(values):
    center = values - jnp.mean(values, -1, keepdims=True)
    inverse = lax.rsqrt(jnp.mean(center * center, -1, keepdims=True) + EPS)
    return center * inverse, inverse


def norm_back(grad_y, normed, inverse, gain):
    scaled = grad_y * gain
    return inverse * (
        scaled
        - jnp.mean(scaled, -1, keepdims=True)
        - normed * jnp.mean(scaled * normed, -1, keepdims=True)
    )


def device_at(kind, rank):
    if kind in ("mp", "ctx"):
        return {kind: rank}
    count = lax.axis_size("ctx")
    return {"batch": rank // count, "ctx": lax.rem(rank, count)}


def remote(src, dst, send, recv, device):
    return pltpu.make_async_remote_copy(
        src_ref=src, dst_ref=dst, send_sem=send, recv_sem=recv,
        device_id=device, device_id_type=MESH,
    )


def colsum(values):
    return jnp.sum(values, 0, keepdims=True)


def run_all(x0, gout, seg, gains, biases, weights, dims):
    (layers, seqs, rows, width, cols, ffc, part, owners, ctx_count, mp_count) = dims
    tokens = seqs * rows
    chips = owners // 2
    piece = width // owners
    heads = cols // HEAD
    stack = heads * rows
    back = (ctx_count * rows // 2 + rows - 2) // rows
    chunks = tokens // CHUNK
    sizes = [w.shape[-1] for w in weights]
    tiles = width // LANES
    group = owners // tiles

    def kernel(
        x0_ref, go_ref, seg_ref, gain_ref, bias_ref, wq_in, wo_in, wu_in, wd_in,
        out_ref, gin_ref, gain_out, bias_out, rq, ro, ru, rd,
        wq, wo, wu, wd, x1, x2, a1, qkv, kvl, ctxs, lse, a2, gs, act,
        part_b, out_a, out_b, land_a, land_b, gy, gyb, gxb, dub, dctx, dqkv, dkv0,
        dkv_out, dkv_in, gq, gw, gu, gd, cq, co, cu, cd,
        vfull, vec_own, qseg, vz, vland, vsum, vecs, kseg, term, tland, tsum, tz, acc, qst, dst,
        loc_sem, wsend, wrecv, fsend, frecv, asend, arecv, bsend, brecv,
        vsend, vrecv, v2send, v2recv, ksend, krecv, gsend, grecv, dsend, drecv,
        csend, crecv, hsend, hrecv, own_sem, t1send, t1recv, t2send, t2recv,
    ):
        me = lax.axis_index("mp")
        here = lax.axis_index("ctx")
        rank = lax.axis_index("batch") * ctx_count + here
        chip = rank // 2
        core = lax.rem(rank, 2)
        sib_rank = chip * 2 + 1 - core
        sibling = device_at("flat", sib_rank)
        side = device_at("mp", me + 1 - 2 * lax.rem(me, 2))
        across = device_at("mp", mp_count - 1 - me)
        is_mid = (me == 1) | (me == 2)
        is_end = (me == 0) | (me == 3)
        zpeers = [device_at("mp", lax.rem(me + t, mp_count)) for t in range(1, mp_count)]
        plane = [device_at("flat", lax.rem(rank + t, owners)) for t in range(1, owners)]
        chip_to = [lax.rem(chip + t, chips) * 2 + core for t in range(1, chips)]
        chip_from = [lax.rem(chip + chips - t, chips) * 2 + core for t in range(1, chips)]
        w_in = [wq_in, wo_in, wu_in, wd_in]
        w_all = [wq, wo, wu, wd]

        def prow(g):
            return pl.ds(pl.multiple_of(g * piece, piece), piece)

        def crow(c):
            return pl.ds(pl.multiple_of(c * CHUNK, CHUNK), CHUNK)

        def srow(s):
            return pl.ds(s * rows, rows)

        def w_rows(l, m, g):
            return w_all[m].at[l, :, prow(g)] if m == 0 else w_all[m].at[l, prow(g)]

        def own_copy(l, m):
            return pltpu.make_async_copy(
                w_in[m].at[l], w_rows(l, m, rank), loc_sem.at[l, m]
            )

        def w_copy(l, m, t, g):
            return remote(
                w_in[m].at[l], w_rows(l, m, g),
                wsend.at[l, m, t], wrecv.at[l, m, t], device_at("flat", chip_to[t]),
            )

        def f_copy(l, m, t, g):
            src = w_in[m].at[l] if t == 0 else w_rows(l, m, g)
            return remote(
                src, w_rows(l, m, g), fsend.at[l, m, t], frecv.at[l, m, t], sibling
            )

        def w_half(l, m, g, h):
            half = piece // 2
            rws = pl.ds(pl.multiple_of(g * piece + h * half, half), half)
            return w_all[m].at[l, :, rws] if m == 0 else w_all[m].at[l, rws]

        square = chips == 4 and piece % 32 == 0
        near = [chip + 2 - 4 * (chip // 2), chip + 1 - 2 * lax.rem(chip, 2)]
        near = [c * 2 + core for c in near]
        far = (chips - 1 - chip) * 2 + core

        def n_copy(l, m, t, g):
            return remote(
                w_in[m].at[l], w_rows(l, m, g),
                wsend.at[l, m, t], wrecv.at[l, m, t], device_at("flat", near[t]),
            )

        def d_copy(l, m, h, g):
            return remote(
                w_half(l, m, g, h), w_half(l, m, g, h),
                wsend.at[l, m, 2 + h], wrecv.at[l, m, 2 + h], device_at("flat", near[1 - h]),
            )

        def w_issue(l, m):
            if square:
                for t in range(2):
                    n_copy(l, m, t, rank).start()
            else:
                for t in range(chips - 1):
                    w_copy(l, m, t, rank).start()
            f_copy(l, m, 0, rank).start()
            own_copy(l, m).start()

        def w_relay(l, m):
            if square:
                for t in range(2):
                    n_copy(l, m, t, near[t]).wait_recv()
                    d_copy(l, m, t, near[t]).start()
                    f_copy(l, m, t + 1, near[t]).start()

        def w_forward(l, m):
            if square:
                for h in range(2):
                    d_copy(l, m, h, far).wait_recv()
                f_copy(l, m, 3, far).start()
            else:
                for t in range(chips - 1):
                    w_copy(l, m, t, chip_from[t]).wait_recv()
                    f_copy(l, m, t + 1, chip_from[t]).start()

        def w_ready(l, m):
            own_copy(l, m).wait()
            f_copy(l, m, 0, sib_rank).wait_recv()
            for t in range(chips - 1):
                source = ([*near, far] if square else chip_from)[t]
                f_copy(l, m, t + 1, source + 1 - 2 * core).wait_recv()

        def w_sent(l, m):
            if square:
                for t in range(2):
                    n_copy(l, m, t, rank).wait_send()
                    d_copy(l, m, t, near[t]).wait_send()
            else:
                for t in range(chips - 1):
                    w_copy(l, m, t, rank).wait_send()

        barrier = pltpu.get_barrier_semaphore()
        for device in zpeers + plane:
            pl.semaphore_signal(barrier, inc=1, device_id=device, device_id_type=MESH)
        pl.semaphore_wait(barrier, len(zpeers) + len(plane))

        w_issue(0, 0)
        offset = lax.rem((rank * mp_count + me) * part, LANES)
        pick = lax.broadcasted_iota(jnp.int32, (part, LANES), 1) == (
            lax.broadcasted_iota(jnp.int32, (part, LANES), 0) + offset
        )
        pick = jnp.where(pick, 1.0, 0.0).astype(BF16)
        vfull[...] = jnp.zeros(vfull.shape, F32)
        for l in range(layers):
            vfull[l * 2 : l * 2 + 2, :] = nn(gain_ref[l], pick)
            low = layers * 2 + l * 10
            vfull[low : low + 10, :] = nn(bias_ref[l], pick)
        vec_own[...] = vfull[...].astype(BF16)

        def vz_copy(t):
            return remote(vec_own, vz.at[t], vsend.at[t], vrecv.at[t], zpeers[t])

        for t in range(mp_count - 1):
            vz_copy(t).start()

        def seg_copy(d):
            return remote(
                seg_ref, kseg.at[d - 1], ksend.at[layers, d - 1, 0], krecv.at[layers, d - 1, 0],
                device_at("ctx", lax.rem(here + d, ctx_count)),
            )

        for d in range(1, back + 1):
            @pl.when(here + d < ctx_count)
            def _():
                seg_copy(d).start()

            @pl.when(here - d < 0)
            def _():
                kseg[d - 1] = jnp.full(kseg.shape[1:], -1, jnp.int32)
                for l in range(layers):
                    kvl[l, d - 1] = jnp.zeros(kvl.shape[2:], BF16)

        vtot = vfull[...]
        for t in range(mp_count - 1):
            vz_copy(t).wait_recv()
            vtot = vtot + vz[t].astype(F32)
        vsum[...] = vtot.astype(BF16)

        def v2_copy(t, g):
            return remote(vsum, vland.at[g], v2send.at[t], v2recv.at[t], plane[t])

        for t in range(owners - 1):
            v2_copy(t, rank).start()
        w_issue(0, 1)
        w_issue(0, 2)
        vland[rank] = vsum[...]
        for t in range(owners - 1):
            v2_copy(t, lax.rem(rank + owners - 1 - t, owners)).wait_recv()
        for t in range(tiles):
            tile = vland[t * group].astype(F32)
            for j in range(1, group):
                tile = tile + vland[t * group + j].astype(F32)
            vecs[:, t * LANES : (t + 1) * LANES] = tile
        term[...] = jnp.zeros(term.shape, F32)
        for d in range(1, back + 1):
            @pl.when(here - d >= 0)
            def _():
                seg_copy(d).wait_recv()

        mine = pl.ds(pl.multiple_of(me * cols, LANES), cols)

        def gain_row(l, i):
            return l * 2 + i

        def bias_row(l, j):
            return layers * 2 + l * 10 + j

        def vrow(r):
            return vecs[r : r + 1, :]

        lane_head = lax.broadcasted_iota(jnp.int32, (rows, cols), 1) // HEAD
        head_lanes = [lane_head == h for h in range(heads)]
        row_i = lax.broadcasted_iota(jnp.int32, (rows, rows), 0)
        col_j = lax.broadcasted_iota(jnp.int32, (rows, rows), 1)
        slopes = [
            jnp.exp2(
                jnp.full((1, rows), -8.0 / HEADS, F32)
                * (me * heads + (h + 1)).astype(F32)
            )
            for h in range(heads)
        ]

        def stacked(ref, values):
            for h in range(heads):
                ref[h * rows : (h + 1) * rows, :] = jnp.where(
                    head_lanes[h], values, jnp.zeros_like(values)
                )

        def block_mask(s, d):
            keys = (seg_ref if d == 0 else kseg.at[d - 1])[s : s + 1, :]
            mask = qseg[s] == keys.astype(F32)
            return mask & (col_j <= row_i) if d == 0 else mask

        for s in range(seqs):
            own = seg_ref[s : s + 1, :].astype(F32)
            qseg[s] = jnp.transpose(jnp.broadcast_to(own, (rows, rows)))

        def block_dist(d):
            return (d * rows + row_i - col_j).astype(F32)

        def key_block(l, s, d):
            if d == 0:
                return qkv[l, srow(s), cols : 2 * cols], qkv[l, srow(s), 2 * cols : 3 * cols]
            return kvl[l, d - 1, srow(s), :cols], kvl[l, d - 1, srow(s), cols:]

        def side_copy(p, c, src):
            return remote(
                src.at[p, crow(c)], land_a.at[p, crow(c)], asend.at[p, c], arecv.at[p, c], side
            )

        def cross_copy(p, c):
            return remote(
                out_b.at[p, crow(c)], land_b.at[p, crow(c)], bsend.at[p, c], brecv.at[p, c], across
            )

        per_seq = rows // CHUNK

        def sum_drain(p, low, high):
            def body(c, carry):
                side_copy(p, c, part_b).wait_send()

                @pl.when(is_mid)
                def _():
                    cross_copy(p, c).wait_send()

                return carry

            lax.fori_loop(low, high, body, 0)

        begun = [0] * seqs

        def sum_begin(s):
            k = begun[s]
            begun[s] += 1
            if k >= 2:
                sum_drain(k % 2, s * per_seq, (s + 1) * per_seq)
            return k % 2

        def sum_start(p, s):
            @pl.when(is_end)
            def _():
                for c in range(s * per_seq, (s + 1) * per_seq):
                    side_copy(p, c, part_b).start()

        def sum_plan(p, consumer):
            def pair_up(c):
                @pl.when(is_mid)
                def _():
                    side_copy(p, c, part_b).wait_recv()
                    pair = part_b[p, crow(c)].astype(F32) + land_a[p, crow(c)].astype(F32)
                    out_b[p, crow(c)] = pair.astype(BF16)
                    cross_copy(p, c).start()

            def close(c):
                @pl.when(is_mid)
                def _():
                    cross_copy(p, c).wait_recv()
                    total = out_b[p, crow(c)].astype(F32) + land_b[p, crow(c)].astype(F32)
                    out_a[p, crow(c)] = total.astype(BF16)
                    side_copy(p, c, out_a).start()

            def use(c):
                @pl.when(is_end)
                def _():
                    side_copy(p, c, part_b).wait_recv()
                    out_a[p, crow(c)] = land_a[p, crow(c)]

                consumer(c, out_a[p, crow(c)].astype(F32))

            pairs = [lambda c=c: pair_up(c) for c in range(chunks)]
            closes = [lambda c=c: close(c) for c in range(chunks)]
            uses = [lambda c=c: use(c) for c in range(chunks)]
            early, wait, host = pairs[:LAG], [], []
            for c in range(per_seq):
                wait += [pairs[c + LAG], closes[c], uses[c]]
            for c in range(per_seq, chunks - 1):
                host += pairs[c + LAG : c + LAG + 1] + [closes[c]]
            return early, wait, host, [closes[-1]] + uses[per_seq:]

        def weave(main, side_steps, lead=0):
            for i, step in enumerate(main):
                step()
                if i >= lead and side_steps:
                    side_steps.pop(0)()

        def finish(side_steps, fillers=(), share=1):
            while side_steps:
                for _ in range(share):
                    if fillers:
                        fillers.pop(0)()
                side_steps.pop(0)()

        def run_steps(fillers):
            while fillers:
                fillers.pop(0)()

        def product_steps(p, s, left, weight):
            def tile(t):
                off = slice(t * 256, (t + 1) * 256)
                part_b[p, srow(s), off] = nt(left(), weight(off)).astype(BF16)

            return [lambda t=t: tile(t) for t in range(width // 256)]

        def kv_copy(l, s, d):
            return remote(
                qkv.at[l, srow(s), pl.ds(cols, 2 * cols)], kvl.at[l, d - 1, srow(s)],
                ksend.at[l, d - 1, s], krecv.at[l, d - 1, s],
                device_at("ctx", lax.rem(here + d, ctx_count)),
            )

        def first_norm(l, rws, x):
            normed, _ = norm_parts(x)
            a1[l, rws] = (normed * vrow(gain_row(l, 0)) + vrow(bias_row(l, 0))).astype(BF16)

        def start_norm(c, carry):
            first_norm(0, crow(c), x0_ref[crow(c)].astype(F32))
            return carry

        lax.fori_loop(0, tokens // CHUNK, start_norm, 0)
        w_relay(0, 0)
        w_issue(0, 3)
        w_forward(0, 0)
        w_ready(0, 0)
        scale = 1.0 / math.sqrt(HEAD)

        def qkv_steps(l, s):
            def kind(u):
                value = nn(a1[l, srow(s)], wq[l, u])
                if u != 1:
                    r = bias_row(l, 2 if u == 0 else 3)
                    value = value + vecs[r : r + 1, mine]
                qkv[l, srow(s), u * cols : (u + 1) * cols] = value.astype(BF16)
                if u == 2:
                    for d in range(1, back + 1):
                        @pl.when(here + d < ctx_count)
                        def _():
                            kv_copy(l, s, d).start()

            return [lambda u=u: kind(u) for u in (1, 2, 0)]

        def attend_steps(l, s):
            totals = [jnp.zeros((rows, 1), F32)] * heads

            def block(d):
                if d == 0:
                    stacked(qst, qkv[l, srow(s), :cols] * BF16(scale))
                else:
                    @pl.when(here - d >= 0)
                    def _():
                        kv_copy(l, s, d).wait_recv()
                keys, values = key_block(l, s, d)
                score = nt(qst[...], keys)
                mask, dist = block_mask(s, d), block_dist(d)
                expos = []
                for h in range(heads):
                    raw = score[h * rows : (h + 1) * rows] - slopes[h] * dist
                    expo = jnp.where(mask, jnp.exp(jnp.where(mask, raw, 0.0)), 0.0)
                    totals[h] = totals[h] + jnp.sum(expo, -1, keepdims=True)
                    expos.append(expo.astype(BF16))
                step = nn(jnp.concatenate(expos, 0), values)
                acc[...] = step if d == 0 else acc[...] + step

            def close():
                out = jnp.zeros((rows, cols), F32)
                for h in range(heads):
                    lse[l * seqs + s, h * rows : (h + 1) * rows, :] = jnp.log(totals[h])
                    out = jnp.where(head_lanes[h], acc[h * rows : (h + 1) * rows, :] / totals[h], out)
                ctxs[l, srow(s)] = out.astype(BF16)

            return [lambda d=d: block(d) for d in range(back + 1)] + [close]

        def mid_norm(l):
            def consumer(c, total):
                base = x0_ref[crow(c)].astype(F32) if l == 0 else x1[crow(c)]
                value = base + total + vrow(bias_row(l, 4))
                x2[l, crow(c)] = value
                normed, _ = norm_parts(value)
                a2[l, crow(c)] = (
                    normed * vrow(gain_row(l, 1)) + vrow(bias_row(l, 1))
                ).astype(BF16)

            return consumer

        def end_norm(l):
            def consumer(c, total):
                value = x2[l, crow(c)] + total + vrow(bias_row(l, 5))
                if l + 1 < layers:
                    x1[crow(c)] = value
                    first_norm(l + 1, crow(c), value)
                else:
                    out_ref[crow(c)] = value.astype(BF16)

            return consumer

        def up_steps(l, s):
            def tile(t):
                off = slice(t * 256, (t + 1) * 256)
                up = nn(a2[l, srow(s)], wu[l, :, off]) + vecs[pl.ds(bias_row(l, 6) + me, 1), off]
                square = up * up
                bend = jnp.tanh(GELU_C * (up + GELU_K * square * up))
                half = 0.5 * (1.0 + bend)
                act[l, srow(s), off] = (up * half).astype(BF16)
                gs[l, srow(s), off] = half + 0.5 * up * (1.0 - bend * bend) * GELU_C * (
                    1.0 + 3.0 * GELU_K * square
                )

            return [lambda t=t: tile(t) for t in range(ffc // 256)]

        first, second = 0, 1

        def forward_layer(l, before):
            host, late = before
            weave(qkv_steps(l, first), host)
            finish(host)
            finish(late)
            w_relay(l, 1)
            weave(qkv_steps(l, second), [])
            w_forward(l, 1)
            w_relay(l, 2)
            if l + 1 < layers:
                w_issue(l + 1, 0)
            p = sum_begin(first)
            steps = attend_steps(l, first) + [lambda: w_ready(l, 1)]
            steps += product_steps(p, first, lambda: ctxs[l, srow(first)], lambda off: wo[l, off, :])
            weave(steps, [])
            sum_start(p, first)
            early, wait, host, late = sum_plan(p, mid_norm(l))
            w_relay(l, 3)
            w_forward(l, 2)
            sum_begin(second)
            steps = attend_steps(l, second)
            steps += product_steps(
                p, second, lambda: ctxs[l, srow(second)], lambda off: wo[l, off, :]
            )
            weave(steps, early, len(steps) - 3)
            sum_start(p, second)
            finish(early)
            w_forward(l, 3)
            if l + 1 < layers:
                w_issue(l + 1, 1)
                w_issue(l + 1, 2)
            finish(wait)
            w_ready(l, 2)
            p = sum_begin(first)
            steps = up_steps(l, first) + [lambda: w_ready(l, 3)]
            steps += product_steps(p, first, lambda: act[l, srow(first)], lambda off: wd[l, off, :])
            weave(steps, host, 2)
            sum_start(p, first)
            finish(host)
            finish(late)
            if l + 1 < layers:
                w_issue(l + 1, 3)
                w_relay(l + 1, 0)
            early, wait, host, late = sum_plan(p, end_norm(l))
            sum_begin(second)
            steps = up_steps(l, second)
            steps += product_steps(p, second, lambda: act[l, srow(second)], lambda off: wd[l, off, :])
            weave(steps, early, len(steps) - 3)
            sum_start(p, second)
            if l + 1 < layers:
                finish(early)
                finish(wait)
                w_forward(l + 1, 0)
                w_ready(l + 1, 0)
                return host, late
            return early + wait + host + late, []

        carried = ([], [])
        for l in range(layers):
            carried = forward_layer(l, carried)

        g_all = [gq, gw, gu, gd]
        c_all = [cq, co, cu, cd]
        r_all = [rq, ro, ru, rd]

        def at_rows(m, rws):
            return (slice(None), rws) if m == 0 else (rws,)

        def c_copy(l, m, q):
            g = q * 2 + 1 - core
            return remote(
                g_all[m].at[at_rows(m, prow(g))],
                c_all[m].at[(l,) + at_rows(m, pl.ds(q * piece, piece))],
                csend.at[l, m, q], crecv.at[l, m, q], sibling,
            )

        def h_copy(l, m, t):
            return remote(
                g_all[m].at[at_rows(m, prow(chip_to[t]))], r_all[m].at[t + 1, l],
                hsend.at[l, m, t], hrecv.at[l, m, t], device_at("flat", chip_to[t]),
            )

        def own_out(l, m):
            return pltpu.make_async_copy(
                g_all[m].at[at_rows(m, prow(rank))], r_all[m].at[0, l], own_sem.at[l, m]
            )

        def share_core(l, m):
            for q in range(chips):
                c_copy(l, m, q).start()

        def share_chip_steps(l, m):
            def add(q):
                c_copy(l, m, q).wait_recv()
                at = at_rows(m, prow(q * 2 + core))
                landed = c_all[m][(l,) + at_rows(m, pl.ds(q * piece, piece))]
                g_all[m][at] = (g_all[m][at].astype(F32) + landed.astype(F32)).astype(BF16)

            def send():
                for t in range(chips - 1):
                    h_copy(l, m, t).start()
                own_out(l, m).start()

            return [lambda q=q: add(q) for q in range(chips)] + [send]

        def share_drain(l, m):
            for q in range(chips):
                c_copy(l, m, q).wait_send()
            for t in range(chips - 1):
                h_copy(l, m, t).wait_send()
            own_out(l, m).wait()

        def share_end(l, m):
            for t in range(chips - 1):
                h_copy(l, m, t).wait_recv()

        def dkv_copy(l, s, d):
            return remote(
                dkv_out.at[d - 1, srow(s)], dkv_in.at[l, d - 1, srow(s)],
                dsend.at[l, d - 1, s], drecv.at[l, d - 1, s],
                device_at("ctx", lax.rem(here + ctx_count - d, ctx_count)),
            )

        def dkv_drain(l):
            for s in range(seqs):
                for d in range(1, back + 1):
                    @pl.when(here - d >= 0)
                    def _():
                        dkv_copy(l, s, d).wait_send()

        def add_term(r, value):
            term[r : r + 1, :] = term[r : r + 1, :] + value

        def unit_steps(l, s):
            last = l == layers - 1

            def cast():
                value = go_ref[srow(s)].astype(F32) if last else gy[srow(s)]
                if last:
                    gy[srow(s)] = value
                gyb[srow(s)] = value.astype(BF16)
                add_term(bias_row(l, 5), colsum(value))

            def tile(t):
                off = slice(t * 256, (t + 1) * 256)
                dup = nn(gyb[srow(s)], wd[l, :, off]) * gs[l, srow(s), off]
                row = pl.ds(bias_row(l, 6) + me, 1)
                term[row, off] = term[row, off] + colsum(dup)
                dub[srow(s), off] = dup.astype(BF16)

            return [cast] + [lambda t=t: tile(t) for t in range(ffc // 256)]

        def second_back(l):
            def consumer(c, total):
                normed, inverse = norm_parts(x2[l, crow(c)])
                add_term(gain_row(l, 1), colsum(total * normed))
                add_term(bias_row(l, 1), colsum(total))
                value = gy[crow(c)] + norm_back(total, normed, inverse, vrow(gain_row(l, 1)))
                add_term(bias_row(l, 4), colsum(value))
                gy[crow(c)] = value
                gxb[crow(c)] = value.astype(BF16)

            return consumer

        def first_back(l):
            def consumer(c, total):
                base = x0_ref[crow(c)].astype(F32) if l == 0 else x1[crow(c)]
                normed, inverse = norm_parts(base)
                add_term(gain_row(l, 0), colsum(total * normed))
                add_term(bias_row(l, 0), colsum(total))
                value = gy[crow(c)] + norm_back(total, normed, inverse, vrow(gain_row(l, 0)))
                if l == 0:
                    gin_ref[crow(c)] = value.astype(BF16)
                else:
                    gy[crow(c)] = value

            return consumer

        def attend_back_steps(l, s):
            deltas = []

            def begin():
                dctx[srow(s)] = nn(gxb[srow(s)], wo[l]).astype(BF16)
                stacked(qst, qkv[l, srow(s), :cols] * BF16(scale))
                stacked(dst, dctx[srow(s), :])
                product = dctx[srow(s), :].astype(F32) * ctxs[l, srow(s)].astype(F32)
                for h in range(heads):
                    deltas.append(
                        jnp.sum(jnp.where(head_lanes[h], product, 0.0), -1, keepdims=True)
                    )

            def block(d):
                keys, values = key_block(l, s, d)
                score = nt(qst[...], keys)
                gprob = nt(dst[...], values)
                mask, dist = block_mask(s, d), block_dist(d)
                probs, gscores = [], []
                for h in range(heads):
                    hrow = slice(h * rows, (h + 1) * rows)
                    raw = score[hrow] - slopes[h] * dist - lse[l * seqs + s, hrow, :]
                    prob = jnp.where(mask, jnp.exp(jnp.where(mask, raw, 0.0)), 0.0)
                    probs.append(prob.astype(BF16))
                    gscores.append((prob * (gprob[hrow] - deltas[h])).astype(BF16))
                probs = jnp.concatenate(probs, 0)
                gscores = jnp.concatenate(gscores, 0)
                gkeys = tn(gscores, qst[...])
                gvalues = tn(probs, dst[...])
                if d:
                    dkv_out[d - 1, srow(s), :cols] = gkeys.astype(BF16)
                    dkv_out[d - 1, srow(s), cols:] = gvalues.astype(BF16)

                    @pl.when(here - d >= 0)
                    def _():
                        dkv_copy(l, s, d).start()
                else:
                    dkv0[srow(s), :cols] = gkeys
                    dkv0[srow(s), cols:] = gvalues
                step = nn(gscores, keys)
                acc[...] = step if d == back else acc[...] + step

            def close():
                out = jnp.zeros((rows, cols), F32)
                for h in range(heads):
                    out = jnp.where(head_lanes[h], acc[h * rows : (h + 1) * rows, :], out)
                out = out * scale
                r = bias_row(l, 2)
                term[r : r + 1, mine] = term[r : r + 1, mine] + colsum(out)
                dqkv[srow(s), :cols] = out.astype(BF16)

            return [begin] + [lambda d=d: block(d) for d in range(back, -1, -1)] + [close]

        def gather_dkv(l, s):
            for d in range(back, 0, -1):
                @pl.when(here + d < ctx_count)
                def _():
                    dkv_copy(l, s, d).wait_recv()
                    dkv0[srow(s), :] = dkv0[srow(s), :] + dkv_in[l, d - 1, srow(s)].astype(F32)
            r = bias_row(l, 3)
            term[r : r + 1, mine] = term[r : r + 1, mine] + colsum(dkv0[srow(s), cols:])
            dqkv[srow(s), cols:] = dkv0[srow(s), :].astype(BF16)

        def in_product_steps(p, l, s):
            def tile(t):
                off = slice(t * 256, (t + 1) * 256)
                value = nt(dqkv[srow(s), :cols], wq[l, 0, off, :])
                for u in (1, 2):
                    value = value + nt(dqkv[srow(s), u * cols : (u + 1) * cols], wq[l, u, off, :])
                part_b[p, srow(s), off] = value.astype(BF16)

            return [lambda t=t: tile(t) for t in range(width // 256)]

        def grad_tiles(one):
            return [lambda c=c: one(slice(c * LANES, (c + 1) * LANES)) for c in range(tiles)]

        def backward_layer(l, before):
            last = l == layers - 1

            def down_grads(off):
                gd[off] = tn(gyb[:, off], act[l]).astype(BF16)

            def up_grads(off):
                gu[off] = tn(a2[l, :, off], dub[...]).astype(BF16)

            def out_grads(off):
                gw[off] = tn(gxb[:, off], ctxs[l]).astype(BF16)

            def in_grads(off):
                for u in range(3):
                    gq[u, off] = tn(
                        a1[l, :, off], dqkv[:, u * cols : (u + 1) * cols]
                    ).astype(BF16)

            host, late = before
            p = sum_begin(first)
            steps = unit_steps(l, first)
            steps += product_steps(p, first, lambda: dub[srow(first)], lambda off: wu[l, off, :])
            weave(steps, host, 3 if last else 1)
            sum_start(p, first)
            finish(host)
            finish(late)
            early, wait, host, late = sum_plan(p, second_back(l))
            sum_begin(second)
            steps = unit_steps(l, second)
            steps += product_steps(p, second, lambda: dub[srow(second)], lambda off: wu[l, off, :])
            weave(steps, early, len(steps) - 3)
            sum_start(p, second)
            finish(early)
            fillers = []
            if not last:
                share_drain(l + 1, 2)
                share_drain(l + 1, 3)
                fillers += share_chip_steps(l + 1, 0) + share_chip_steps(l + 1, 1)
            fillers += grad_tiles(down_grads) + [lambda: share_core(l, 3)]
            fillers += grad_tiles(up_grads) + [lambda: share_core(l, 2)]
            finish(wait, fillers)
            if not last:
                dkv_drain(l + 1)
            weave(attend_back_steps(l, first), host)
            finish(host, fillers)
            finish(late, fillers)
            run_steps(fillers)
            steps = attend_back_steps(l, second)
            steps[-2:] = share_chip_steps(l, 3) + steps[-2:] + share_chip_steps(l, 2)
            run_steps(steps)
            if not last:
                share_drain(l + 1, 0)
                share_drain(l + 1, 1)
            gather_dkv(l, first)
            p = sum_begin(first)
            run_steps(in_product_steps(p, l, first))
            sum_start(p, first)
            early, wait, host, late = sum_plan(p, first_back(l))
            gather_dkv(l, second)
            sum_begin(second)
            steps = in_product_steps(p, l, second)
            weave(steps, early, len(steps) - 2)
            sum_start(p, second)
            finish(early)
            fillers = grad_tiles(out_grads) + [lambda: share_core(l, 1)]
            fillers += grad_tiles(in_grads) + [lambda: share_core(l, 0)]
            finish(wait, fillers, 2)
            run_steps(fillers)
            if l:
                return host, late
            fillers = share_chip_steps(0, 1) + share_chip_steps(0, 0)
            finish(host, fillers)
            finish(late, fillers)
            run_steps(fillers)

        for l in reversed(range(layers)):
            carried = backward_layer(l, carried)

        alike = [gain_row(l, i) for l in range(layers) for i in range(2)] + [
            bias_row(l, j) for l in range(layers) for j in (0, 1, 4, 5)
        ]

        @pl.when(me != 0)
        def _():
            for r in alike:
                term[r : r + 1, :] = jnp.zeros((1, width), F32)

        def t1_copy(t, g):
            to = lax.rem(rank + t + 1, owners)
            tile = pl.ds(pl.multiple_of((to // group) * LANES, LANES), LANES)
            return remote(term.at[:, tile], tland.at[g], t1send.at[t], t1recv.at[t], plane[t])

        def t2_copy(t):
            return remote(tsum, tz.at[t], t2send.at[t], t2recv.at[t], zpeers[t])

        for t in range(owners - 1):
            t1_copy(t, rank).start()
        own_tile = pl.ds(pl.multiple_of((rank // group) * LANES, LANES), LANES)
        total = term[:, own_tile]
        for t in range(owners - 1):
            source = lax.rem(rank + owners - 1 - t, owners)
            t1_copy(t, source).wait_recv()
            total = total + tland[source]
        tsum[...] = total
        for t in range(mp_count - 1):
            t2_copy(t).start()
        for t in range(mp_count - 1):
            t2_copy(t).wait_recv()
            total = total + tz[t]
        total = pltpu.roll(total, lax.rem(LANES - offset, LANES), 1)
        for l in range(layers):
            gain_out[l] = total[l * 2 : l * 2 + 2, :part]
            low = layers * 2 + l * 10
            bias_out[l] = total[low : low + 10, :part]

        for m in range(4):
            share_drain(0, m)
            for l in range(layers):
                share_end(l, m)
                w_sent(l, m)
                for t in range(chips):
                    f_copy(l, m, t, rank).wait_send()
        dkv_drain(0)
        sum_drain(0, 0, tokens // CHUNK)
        sum_drain(1, 0, tokens // CHUNK)
        for t in range(mp_count - 1):
            vz_copy(t).wait_send()
            t2_copy(t).wait_send()
        for t in range(owners - 1):
            v2_copy(t, rank).wait_send()
            t1_copy(t, rank).wait_send()
        for d in range(1, back + 1):
            @pl.when(here + d < ctx_count)
            def _():
                seg_copy(d).wait_send()
                for l in range(layers):
                    for s in range(seqs):
                        kv_copy(l, s, d).wait_send()

    def vm(*shape, dtype=BF16):
        return pltpu.VMEM(shape, dtype)

    def dma(*shape):
        return pltpu.SemaphoreType.DMA(shape)

    scratch = [vm(layers, 3, width, cols)] + [vm(layers, width, n) for n in sizes[1:]]
    scratch += [
        vm(tokens, width, dtype=F32),
        vm(layers, tokens, width, dtype=F32),
        vm(layers, tokens, width),
        vm(layers, tokens, 3 * cols),
        vm(layers, back, tokens, 2 * cols),
        vm(layers, tokens, cols),
        vm(layers * seqs, stack, 1, dtype=F32),
        vm(layers, tokens, width),
        vm(layers, tokens, ffc, dtype=F32),
        vm(layers, tokens, ffc),
    ]
    scratch += [vm(2, tokens, width)] * 5
    scratch += [
        vm(tokens, width, dtype=F32),
        vm(tokens, width),
        vm(tokens, width),
        vm(tokens, ffc),
        vm(tokens, cols),
        vm(tokens, 3 * cols),
        vm(tokens, 2 * cols, dtype=F32),
        vm(back, tokens, 2 * cols),
        vm(layers, back, tokens, 2 * cols),
    ]
    scratch += [vm(3, width, cols)] + [vm(width, n) for n in sizes[1:]]
    scratch += [vm(layers, 3, width // 2, cols)]
    scratch += [vm(layers, width // 2, n) for n in sizes[1:]]
    scratch += [
        vm(VEC_ROWS, LANES, dtype=F32),
        vm(VEC_ROWS, LANES),
        vm(seqs, rows, rows, dtype=F32),
        vm(mp_count - 1, VEC_ROWS, LANES),
        vm(owners, VEC_ROWS, LANES),
        vm(VEC_ROWS, LANES),
        vm(VEC_ROWS, width, dtype=F32),
        vm(back, seqs, rows, dtype=jnp.int32),
        vm(VEC_ROWS, width, dtype=F32),
        vm(owners, VEC_ROWS, LANES, dtype=F32),
        vm(VEC_ROWS, LANES, dtype=F32),
        vm(mp_count - 1, VEC_ROWS, LANES, dtype=F32),
        vm(stack, cols, dtype=F32),
        vm(stack, cols),
        vm(stack, cols),
    ]
    scratch += [
        dma(layers, 4),
        dma(layers, 4, max(4, chips)), dma(layers, 4, max(4, chips)),
        dma(layers, 4, chips), dma(layers, 4, chips),
        dma(2, chunks), dma(2, chunks), dma(2, chunks), dma(2, chunks),
        dma(mp_count - 1), dma(mp_count - 1),
        dma(owners - 1), dma(owners - 1),
        dma(layers + 1, back, seqs), dma(layers + 1, back, seqs),
        dma(1), dma(1),
        dma(layers, back, seqs), dma(layers, back, seqs),
        dma(layers, 4, chips), dma(layers, 4, chips),
        dma(layers, 4, chips - 1), dma(layers, 4, chips - 1),
        dma(layers, 4),
        dma(owners - 1), dma(owners - 1),
        dma(mp_count - 1), dma(mp_count - 1),
    ]
    return pl.pallas_call(
        kernel,
        out_shape=[
            jax.ShapeDtypeStruct((tokens, width), BF16),
            jax.ShapeDtypeStruct((tokens, width), BF16),
            jax.ShapeDtypeStruct((layers, 2, part), F32),
            jax.ShapeDtypeStruct((layers, 10, part), F32),
        ]
        + [jax.ShapeDtypeStruct((chips,) + w.shape, BF16) for w in weights],
        in_specs=[VMEM] * 5 + [ANY] * 4,
        out_specs=[VMEM] * 4 + [ANY] * 4,
        scratch_shapes=scratch,
        compiler_params=pltpu.CompilerParams(
            collective_id=0, has_side_effects=True, vmem_limit_bytes=62 * 1024 * 1024
        ),
        name="both_layers",
    )(x0, gout, seg, gains, biases, *weights)


def per_device(hidden_in, segment_ids, gains, biases, w_qkv, w_out_t, w_up, w_down_t, grad_out):
    seqs, rows, width = hidden_in.shape
    layers = w_qkv.shape[0]
    cols = w_qkv.shape[3]
    ffc = w_up.shape[2]
    piece = w_qkv.shape[1]
    part = gains.shape[2]
    ctx_count = lax.axis_size("ctx")
    mp_count = lax.axis_size("mp")
    owners = lax.axis_size("batch") * ctx_count
    dims = (layers, seqs, rows, width, cols, ffc, part, owners, ctx_count, mp_count)
    output, grad_in, grad_gains, grad_biases, gq, go, gu, gd = run_all(
        hidden_in.reshape(seqs * rows, width),
        grad_out.reshape(seqs * rows, width),
        segment_ids, gains, biases,
        [jnp.transpose(w_qkv, (0, 2, 1, 3)), w_out_t, w_up, w_down_t],
        dims,
    )
    def total(slots):
        acc = slots[0].astype(F32)
        for t in range(1, slots.shape[0]):
            acc = acc + slots[t].astype(F32)
        return acc

    return (
        output.reshape(hidden_in.shape),
        grad_in.reshape(hidden_in.shape),
        grad_gains,
        grad_biases,
        jnp.transpose(total(gq), (0, 2, 1, 3)),
        total(go),
        total(gu),
        total(gd),
    )


def solution(mesh):
    in_specs = (
        P("batch", "ctx", None),
        P("batch", "ctx"),
        P(None, None, ("batch", "ctx", "mp")),
        P(None, None, ("batch", "ctx", "mp")),
        P(None, ("batch", "ctx"), None, "mp"),
        P(None, ("batch", "ctx"), "mp"),
        P(None, ("batch", "ctx"), "mp"),
        P(None, ("batch", "ctx"), "mp"),
        P("batch", "ctx", None),
    )
    out_specs = (
        P("batch", "ctx", None),
        P("batch", "ctx", None),
        P(None, None, ("batch", "ctx", "mp")),
        P(None, None, ("batch", "ctx", "mp")),
        P(None, ("batch", "ctx"), None, "mp"),
        P(None, ("batch", "ctx"), "mp"),
        P(None, ("batch", "ctx"), "mp"),
        P(None, ("batch", "ctx"), "mp"),
    )
    return jax.shard_map(
        per_device, mesh=mesh, in_specs=in_specs, out_specs=out_specs, check_vma=False
    )
```

```python
import math

import jax
import jax.numpy as jnp
from jax import lax
from jax.experimental import pallas as pl
from jax.experimental.pallas import tpu as pltpu
from jax.sharding import PartitionSpec as P

HEADS = 16
HEAD = 64
EPS = 1e-05
GELU_C = 0.7978845608028654
GELU_K = 0.044715
LANES = 128
VEC_ROWS = 32
CHUNK = 32
LAG = 2
F32 = jnp.float32
BF16 = jnp.bfloat16

MESH = pl.DeviceIdType.MESH
ANY = pl.BlockSpec(memory_space=pl.ANY)
VMEM = pl.BlockSpec(memory_space=pltpu.VMEM)


def nn(a, b):
    return lax.dot_general(a, b, (((1,), (0,)), ((), ())), preferred_element_type=F32)


def nt(a, b):
    return lax.dot_general(a, b, (((1,), (1,)), ((), ())), preferred_element_type=F32)


def tn(a, b):
    return lax.dot_general(a, b, (((0,), (0,)), ((), ())), preferred_element_type=F32)


def norm_parts(values):
    center = values - jnp.mean(values, -1, keepdims=True)
    inverse = lax.rsqrt(jnp.mean(center * center, -1, keepdims=True) + EPS)
    return center * inverse, inverse


def norm_back(grad_y, normed, inverse, gain):
    scaled = grad_y * gain
    return inverse * (
        scaled
        - jnp.mean(scaled, -1, keepdims=True)
        - normed * jnp.mean(scaled * normed, -1, keepdims=True)
    )


def device_at(kind, rank):
    if kind in ("mp", "ctx"):
        return {kind: rank}
    count = lax.axis_size("ctx")
    return {"batch": rank // count, "ctx": lax.rem(rank, count)}


def remote(src, dst, send, recv, device):
    return pltpu.make_async_remote_copy(
        src_ref=src, dst_ref=dst, send_sem=send, recv_sem=recv,
        device_id=device, device_id_type=MESH,
    )


def colsum(values):
    return jnp.sum(values, 0, keepdims=True)


def run_all(x0, gout, seg, gains, biases, weights, dims):
    (layers, seqs, rows, width, cols, ffc, part, owners, ctx_count, mp_count) = dims
    tokens = seqs * rows
    chips = owners // 2
    piece = width // owners
    heads = cols // HEAD
    stack = heads * rows
    back = (ctx_count * rows // 2 + rows - 2) // rows
    chunks = tokens // CHUNK
    sizes = [w.shape[-1] for w in weights]
    tiles = width // LANES
    group = owners // tiles

    def kernel(
        x0_ref, go_ref, seg_ref, gain_ref, bias_ref, wq_in, wo_in, wu_in, wd_in,
        out_ref, gin_ref, gain_out, bias_out, rq, ro, ru, rd,
        wq, wo, wu, wd, x1, x2, a1, qkv, kvl, ctxs, lse, a2, gs, act,
        part_b, out_a, out_b, land_a, land_b, gy, gyb, gxb, dub, dctx, dqkv, dkv0,
        dkv_out, dkv_in, gq, gw, gu, gd, cq, co, cu, cd, eq, eo, eu, ed,
        vfull, vec_own, qseg, vz, vland, vsum, vecs, kseg, term, tland, tsum, tz, acc, qst, dst,
        loc_sem, wsend, wrecv, fsend, frecv, asend, arecv, bsend, brecv,
        vsend, vrecv, v2send, v2recv, ksend, krecv, gsend, grecv, dsend, drecv,
        csend, crecv, hsend, hrecv, own_sem, t1send, t1recv, t2send, t2recv,
    ):
        me = lax.axis_index("mp")
        here = lax.axis_index("ctx")
        rank = lax.axis_index("batch") * ctx_count + here
        chip = rank // 2
        core = lax.rem(rank, 2)
        sib_rank = chip * 2 + 1 - core
        sibling = device_at("flat", sib_rank)
        side = device_at("mp", me + 1 - 2 * lax.rem(me, 2))
        across = device_at("mp", mp_count - 1 - me)
        is_mid = (me == 1) | (me == 2)
        is_end = (me == 0) | (me == 3)
        zpeers = [device_at("mp", lax.rem(me + t, mp_count)) for t in range(1, mp_count)]
        plane = [device_at("flat", lax.rem(rank + t, owners)) for t in range(1, owners)]
        chip_to = [lax.rem(chip + t, chips) * 2 + core for t in range(1, chips)]
        chip_from = [lax.rem(chip + chips - t, chips) * 2 + core for t in range(1, chips)]
        w_in = [wq_in, wo_in, wu_in, wd_in]
        w_all = [wq, wo, wu, wd]

        def prow(g):
            return pl.ds(pl.multiple_of(g * piece, piece), piece)

        def crow(c):
            return pl.ds(pl.multiple_of(c * CHUNK, CHUNK), CHUNK)

        def srow(s):
            return pl.ds(s * rows, rows)

        def w_rows(l, m, g):
            return w_all[m].at[l, :, prow(g)] if m == 0 else w_all[m].at[l, prow(g)]

        def own_copy(l, m):
            return pltpu.make_async_copy(
                w_in[m].at[l], w_rows(l, m, rank), loc_sem.at[l, m]
            )

        def w_copy(l, m, t, g):
            return remote(
                w_in[m].at[l], w_rows(l, m, g),
                wsend.at[l, m, t], wrecv.at[l, m, t], device_at("flat", chip_to[t]),
            )

        def f_copy(l, m, t, g):
            src = w_in[m].at[l] if t == 0 else w_rows(l, m, g)
            return remote(
                src, w_rows(l, m, g), fsend.at[l, m, t], frecv.at[l, m, t], sibling
            )

        def w_half(l, m, g, h):
            half = piece // 2
            rws = pl.ds(pl.multiple_of(g * piece + h * half, half), half)
            return w_all[m].at[l, :, rws] if m == 0 else w_all[m].at[l, rws]

        square = chips == 4 and piece % 32 == 0
        near = [chip + 2 - 4 * (chip // 2), chip + 1 - 2 * lax.rem(chip, 2)]
        near = [c * 2 + core for c in near]
        far = (chips - 1 - chip) * 2 + core

        def n_copy(l, m, t, g):
            return remote(
                w_in[m].at[l], w_rows(l, m, g),
                wsend.at[l, m, t], wrecv.at[l, m, t], device_at("flat", near[t]),
            )

        def d_copy(l, m, h, g):
            return remote(
                w_half(l, m, g, h), w_half(l, m, g, h),
                wsend.at[l, m, 2 + h], wrecv.at[l, m, 2 + h], device_at("flat", near[1 - h]),
            )

        def w_issue(l, m):
            if square:
                for t in range(2):
                    n_copy(l, m, t, rank).start()
            else:
                for t in range(chips - 1):
                    w_copy(l, m, t, rank).start()
            f_copy(l, m, 0, rank).start()
            own_copy(l, m).start()

        def w_relay(l, m):
            if square:
                for t in range(2):
                    n_copy(l, m, t, near[t]).wait_recv()
                    d_copy(l, m, t, near[t]).start()
                    f_copy(l, m, t + 1, near[t]).start()

        def w_forward(l, m):
            if square:
                for h in range(2):
                    d_copy(l, m, h, far).wait_recv()
                f_copy(l, m, 3, far).start()
            else:
                for t in range(chips - 1):
                    w_copy(l, m, t, chip_from[t]).wait_recv()
                    f_copy(l, m, t + 1, chip_from[t]).start()

        def w_ready(l, m):
            own_copy(l, m).wait()
            f_copy(l, m, 0, sib_rank).wait_recv()
            for t in range(chips - 1):
                source = ([*near, far] if square else chip_from)[t]
                f_copy(l, m, t + 1, source + 1 - 2 * core).wait_recv()

        def w_sent(l, m):
            if square:
                for t in range(2):
                    n_copy(l, m, t, rank).wait_send()
                    d_copy(l, m, t, near[t]).wait_send()
            else:
                for t in range(chips - 1):
                    w_copy(l, m, t, rank).wait_send()

        barrier = pltpu.get_barrier_semaphore()
        for device in zpeers + plane:
            pl.semaphore_signal(barrier, inc=1, device_id=device, device_id_type=MESH)
        pl.semaphore_wait(barrier, len(zpeers) + len(plane))

        w_issue(0, 0)
        offset = lax.rem((rank * mp_count + me) * part, LANES)
        pick = lax.broadcasted_iota(jnp.int32, (part, LANES), 1) == (
            lax.broadcasted_iota(jnp.int32, (part, LANES), 0) + offset
        )
        pick = jnp.where(pick, 1.0, 0.0).astype(BF16)
        vfull[...] = jnp.zeros(vfull.shape, F32)
        for l in range(layers):
            vfull[l * 2 : l * 2 + 2, :] = nn(gain_ref[l], pick)
            low = layers * 2 + l * 10
            vfull[low : low + 10, :] = nn(bias_ref[l], pick)
        vec_own[...] = vfull[...].astype(BF16)

        def vz_copy(t):
            return remote(vec_own, vz.at[t], vsend.at[t], vrecv.at[t], zpeers[t])

        for t in range(mp_count - 1):
            vz_copy(t).start()

        def seg_copy(d):
            return remote(
                seg_ref, kseg.at[d - 1], ksend.at[layers, d - 1, 0], krecv.at[layers, d - 1, 0],
                device_at("ctx", lax.rem(here + d, ctx_count)),
            )

        for d in range(1, back + 1):
            @pl.when(here + d < ctx_count)
            def _():
                seg_copy(d).start()

            @pl.when(here - d < 0)
            def _():
                kseg[d - 1] = jnp.full(kseg.shape[1:], -1, jnp.int32)
                for l in range(layers):
                    kvl[l, d - 1] = jnp.zeros(kvl.shape[2:], BF16)

        vtot = vfull[...]
        for t in range(mp_count - 1):
            vz_copy(t).wait_recv()
            vtot = vtot + vz[t].astype(F32)
        vsum[...] = vtot.astype(BF16)

        def v2_copy(t, g):
            return remote(vsum, vland.at[g], v2send.at[t], v2recv.at[t], plane[t])

        for t in range(owners - 1):
            v2_copy(t, rank).start()
        w_issue(0, 1)
        w_issue(0, 2)
        vland[rank] = vsum[...]
        for t in range(owners - 1):
            v2_copy(t, lax.rem(rank + owners - 1 - t, owners)).wait_recv()
        for t in range(tiles):
            tile = vland[t * group].astype(F32)
            for j in range(1, group):
                tile = tile + vland[t * group + j].astype(F32)
            vecs[:, t * LANES : (t + 1) * LANES] = tile
        term[...] = jnp.zeros(term.shape, F32)
        for d in range(1, back + 1):
            @pl.when(here - d >= 0)
            def _():
                seg_copy(d).wait_recv()

        mine = pl.ds(pl.multiple_of(me * cols, LANES), cols)

        def gain_row(l, i):
            return l * 2 + i

        def bias_row(l, j):
            return layers * 2 + l * 10 + j

        def vrow(r):
            return vecs[r : r + 1, :]

        lane_head = lax.broadcasted_iota(jnp.int32, (rows, cols), 1) // HEAD
        head_lanes = [lane_head == h for h in range(heads)]
        row_i = lax.broadcasted_iota(jnp.int32, (rows, rows), 0)
        col_j = lax.broadcasted_iota(jnp.int32, (rows, rows), 1)
        slopes = [
            jnp.exp2(
                jnp.full((1, rows), -8.0 / HEADS, F32)
                * (me * heads + (h + 1)).astype(F32)
            )
            for h in range(heads)
        ]

        def stacked(ref, values):
            for h in range(heads):
                ref[h * rows : (h + 1) * rows, :] = jnp.where(
                    head_lanes[h], values, jnp.zeros_like(values)
                )

        def block_mask(s, d):
            keys = (seg_ref if d == 0 else kseg.at[d - 1])[s : s + 1, :]
            mask = qseg[s] == keys.astype(F32)
            return mask & (col_j <= row_i) if d == 0 else mask

        for s in range(seqs):
            own = seg_ref[s : s + 1, :].astype(F32)
            qseg[s] = jnp.transpose(jnp.broadcast_to(own, (rows, rows)))

        def block_dist(d):
            return (d * rows + row_i - col_j).astype(F32)

        def key_block(l, s, d):
            if d == 0:
                return qkv[l, srow(s), cols : 2 * cols], qkv[l, srow(s), 2 * cols : 3 * cols]
            return kvl[l, d - 1, srow(s), :cols], kvl[l, d - 1, srow(s), cols:]

        def side_copy(p, c, src):
            return remote(
                src.at[p, crow(c)], land_a.at[p, crow(c)], asend.at[p, c], arecv.at[p, c], side
            )

        def cross_copy(p, c):
            return remote(
                out_b.at[p, crow(c)], land_b.at[p, crow(c)], bsend.at[p, c], brecv.at[p, c], across
            )

        per_seq = rows // CHUNK

        def sum_drain(p, low, high):
            def body(c, carry):
                side_copy(p, c, part_b).wait_send()

                @pl.when(is_mid)
                def _():
                    cross_copy(p, c).wait_send()

                return carry

            lax.fori_loop(low, high, body, 0)

        begun = [0] * seqs

        def sum_begin(s):
            k = begun[s]
            begun[s] += 1
            if k >= 2:
                sum_drain(k % 2, s * per_seq, (s + 1) * per_seq)
            return k % 2

        def sum_start(p, s):
            @pl.when(is_end)
            def _():
                for c in range(s * per_seq, (s + 1) * per_seq):
                    side_copy(p, c, part_b).start()

        def sum_plan(p, consumer):
            def pair_up(c):
                @pl.when(is_mid)
                def _():
                    side_copy(p, c, part_b).wait_recv()
                    pair = part_b[p, crow(c)].astype(F32) + land_a[p, crow(c)].astype(F32)
                    out_b[p, crow(c)] = pair.astype(BF16)
                    cross_copy(p, c).start()

            def close(c):
                @pl.when(is_mid)
                def _():
                    cross_copy(p, c).wait_recv()
                    total = out_b[p, crow(c)].astype(F32) + land_b[p, crow(c)].astype(F32)
                    out_a[p, crow(c)] = total.astype(BF16)
                    side_copy(p, c, out_a).start()

            def use(c):
                @pl.when(is_end)
                def _():
                    side_copy(p, c, part_b).wait_recv()
                    out_a[p, crow(c)] = land_a[p, crow(c)]

                consumer(c, out_a[p, crow(c)].astype(F32))

            pairs = [lambda c=c: pair_up(c) for c in range(chunks)]
            closes = [lambda c=c: close(c) for c in range(chunks)]
            uses = [lambda c=c: use(c) for c in range(chunks)]
            early, wait, host = pairs[:LAG], [], []
            for c in range(per_seq):
                wait += [pairs[c + LAG], closes[c], uses[c]]
            for c in range(per_seq, chunks - 1):
                host += pairs[c + LAG : c + LAG + 1] + [closes[c]]
            return early, wait, host, [closes[-1]] + uses[per_seq:]

        def weave(main, side_steps, lead=0):
            for i, step in enumerate(main):
                step()
                if i >= lead and side_steps:
                    side_steps.pop(0)()

        def finish(side_steps, fillers=(), share=1):
            while side_steps:
                for _ in range(share):
                    if fillers:
                        fillers.pop(0)()
                side_steps.pop(0)()

        def run_steps(fillers):
            while fillers:
                fillers.pop(0)()

        def product_steps(p, s, left, weight):
            def tile(t):
                off = slice(t * 256, (t + 1) * 256)
                part_b[p, srow(s), off] = nt(left(), weight(off)).astype(BF16)

            return [lambda t=t: tile(t) for t in range(width // 256)]

        def kv_copy(l, s, d):
            return remote(
                qkv.at[l, srow(s), pl.ds(cols, 2 * cols)], kvl.at[l, d - 1, srow(s)],
                ksend.at[l, d - 1, s], krecv.at[l, d - 1, s],
                device_at("ctx", lax.rem(here + d, ctx_count)),
            )

        def first_norm(l, rws, x):
            normed, _ = norm_parts(x)
            a1[l, rws] = (normed * vrow(gain_row(l, 0)) + vrow(bias_row(l, 0))).astype(BF16)

        def start_norm(c, carry):
            first_norm(0, crow(c), x0_ref[crow(c)].astype(F32))
            return carry

        lax.fori_loop(0, tokens // CHUNK, start_norm, 0)
        w_relay(0, 0)
        w_issue(0, 3)
        w_forward(0, 0)
        w_ready(0, 0)
        scale = 1.0 / math.sqrt(HEAD)

        def qkv_steps(l, s):
            def kind(u):
                value = nn(a1[l, srow(s)], wq[l, u])
                if u != 1:
                    r = bias_row(l, 2 if u == 0 else 3)
                    value = value + vecs[r : r + 1, mine]
                qkv[l, srow(s), u * cols : (u + 1) * cols] = value.astype(BF16)
                if u == 2:
                    for d in range(1, back + 1):
                        @pl.when(here + d < ctx_count)
                        def _():
                            kv_copy(l, s, d).start()

            return [lambda u=u: kind(u) for u in (1, 2, 0)]

        def attend_steps(l, s):
            totals = [jnp.zeros((rows, 1), F32)] * heads

            def block(d):
                if d == 0:
                    stacked(qst, qkv[l, srow(s), :cols] * BF16(scale))
                else:
                    @pl.when(here - d >= 0)
                    def _():
                        kv_copy(l, s, d).wait_recv()
                keys, values = key_block(l, s, d)
                score = nt(qst[...], keys)
                mask, dist = block_mask(s, d), block_dist(d)
                expos = []
                for h in range(heads):
                    raw = score[h * rows : (h + 1) * rows] - slopes[h] * dist
                    expo = jnp.where(mask, jnp.exp(jnp.where(mask, raw, 0.0)), 0.0)
                    totals[h] = totals[h] + jnp.sum(expo, -1, keepdims=True)
                    expos.append(expo.astype(BF16))
                step = nn(jnp.concatenate(expos, 0), values)
                acc[...] = step if d == 0 else acc[...] + step

            def close():
                out = jnp.zeros((rows, cols), F32)
                for h in range(heads):
                    lse[l * seqs + s, h * rows : (h + 1) * rows, :] = jnp.log(totals[h])
                    out = jnp.where(head_lanes[h], acc[h * rows : (h + 1) * rows, :] / totals[h], out)
                ctxs[l, srow(s)] = out.astype(BF16)

            return [lambda d=d: block(d) for d in range(back + 1)] + [close]

        def mid_norm(l):
            def consumer(c, total):
                base = x0_ref[crow(c)].astype(F32) if l == 0 else x1[crow(c)]
                value = base + total + vrow(bias_row(l, 4))
                x2[l, crow(c)] = value
                normed, _ = norm_parts(value)
                a2[l, crow(c)] = (
                    normed * vrow(gain_row(l, 1)) + vrow(bias_row(l, 1))
                ).astype(BF16)

            return consumer

        def end_norm(l):
            def consumer(c, total):
                value = x2[l, crow(c)] + total + vrow(bias_row(l, 5))
                if l + 1 < layers:
                    x1[crow(c)] = value
                    first_norm(l + 1, crow(c), value)
                else:
                    out_ref[crow(c)] = value.astype(BF16)

            return consumer

        def up_steps(l, s):
            def tile(t):
                off = slice(t * 256, (t + 1) * 256)
                up = nn(a2[l, srow(s)], wu[l, :, off]) + vecs[pl.ds(bias_row(l, 6) + me, 1), off]
                square = up * up
                bend = jnp.tanh(GELU_C * (up + GELU_K * square * up))
                half = 0.5 * (1.0 + bend)
                act[l, srow(s), off] = (up * half).astype(BF16)
                gs[l, srow(s), off] = half + 0.5 * up * (1.0 - bend * bend) * GELU_C * (
                    1.0 + 3.0 * GELU_K * square
                )

            return [lambda t=t: tile(t) for t in range(ffc // 256)]

        first, second = 0, 1

        def forward_layer(l, before):
            host, late = before
            weave(qkv_steps(l, first), host)
            finish(host)
            finish(late)
            w_relay(l, 1)
            weave(qkv_steps(l, second), [])
            w_forward(l, 1)
            w_relay(l, 2)
            if l + 1 < layers:
                w_issue(l + 1, 0)
            p = sum_begin(first)
            steps = attend_steps(l, first) + [lambda: w_ready(l, 1)]
            steps += product_steps(p, first, lambda: ctxs[l, srow(first)], lambda off: wo[l, off, :])
            weave(steps, [])
            sum_start(p, first)
            early, wait, host, late = sum_plan(p, mid_norm(l))
            w_relay(l, 3)
            w_forward(l, 2)
            sum_begin(second)
            steps = attend_steps(l, second)
            steps += product_steps(
                p, second, lambda: ctxs[l, srow(second)], lambda off: wo[l, off, :]
            )
            weave(steps, early, len(steps) - 3)
            sum_start(p, second)
            finish(early)
            w_forward(l, 3)
            if l + 1 < layers:
                w_issue(l + 1, 1)
                w_issue(l + 1, 2)
            finish(wait)
            w_ready(l, 2)
            p = sum_begin(first)
            steps = up_steps(l, first) + [lambda: w_ready(l, 3)]
            steps += product_steps(p, first, lambda: act[l, srow(first)], lambda off: wd[l, off, :])
            weave(steps, host, 2)
            sum_start(p, first)
            finish(host)
            finish(late)
            if l + 1 < layers:
                w_issue(l + 1, 3)
                w_relay(l + 1, 0)
            early, wait, host, late = sum_plan(p, end_norm(l))
            sum_begin(second)
            steps = up_steps(l, second)
            steps += product_steps(p, second, lambda: act[l, srow(second)], lambda off: wd[l, off, :])
            weave(steps, early, len(steps) - 3)
            sum_start(p, second)
            if l + 1 < layers:
                finish(early)
                finish(wait)
                w_forward(l + 1, 0)
                w_ready(l + 1, 0)
                return host, late
            return early + wait + host + late, []

        carried = ([], [])
        for l in range(layers):
            carried = forward_layer(l, carried)

        g_all = [gq, gw, gu, gd]
        c_all = [cq, co, cu, cd]
        r_all = [rq, ro, ru, rd]
        e_all = [eq, eo, eu, ed]

        def at_rows(m, rws):
            return (slice(None), rws) if m == 0 else (rws,)

        def c_copy(l, m, q):
            g = q * 2 + 1 - core
            return remote(
                g_all[m].at[at_rows(m, prow(g))],
                c_all[m].at[(l,) + at_rows(m, pl.ds(q * piece, piece))],
                csend.at[l, m, q], crecv.at[l, m, q], sibling,
            )

        def h_copy(l, m, t):
            return remote(
                g_all[m].at[at_rows(m, prow(chip_to[t]))], r_all[m].at[t + 1, l],
                hsend.at[l, m, t], hrecv.at[l, m, t], device_at("flat", chip_to[t]),
            )

        def half_rows(m, g, h):
            half = piece // 2
            return at_rows(m, pl.ds(pl.multiple_of(g * piece + h * half, half), half))

        def e_copy(l, m, h, g):
            return remote(
                g_all[m].at[half_rows(m, g, h)], e_all[m].at[l, h],
                hsend.at[l, m, h], hrecv.at[l, m, h], device_at("flat", near[h]),
            )

        def b_copy(l, m, t):
            return remote(
                g_all[m].at[at_rows(m, prow(near[t]))], r_all[m].at[t + 1, l],
                hsend.at[l, m, 2 + t], hrecv.at[l, m, 2 + t], device_at("flat", near[t]),
            )

        def own_out(l, m):
            return pltpu.make_async_copy(
                g_all[m].at[at_rows(m, prow(rank))], r_all[m].at[0, l], own_sem.at[l, m]
            )

        def share_core(l, m):
            for q in range(chips):
                c_copy(l, m, q).start()

        def share_chip_steps(l, m):
            def add(q):
                c_copy(l, m, q).wait_recv()
                at = at_rows(m, prow(q * 2 + core))
                landed = c_all[m][(l,) + at_rows(m, pl.ds(q * piece, piece))]
                g_all[m][at] = (g_all[m][at].astype(F32) + landed.astype(F32)).astype(BF16)

            def send():
                if square:
                    for h in range(2):
                        e_copy(l, m, h, far).start()
                else:
                    for t in range(chips - 1):
                        h_copy(l, m, t).start()
                own_out(l, m).start()

            return [lambda q=q: add(q) for q in range(chips)] + [send]

        def share_relay(l, m):
            if square:
                for h in range(2):
                    e_copy(l, m, h, far).wait_recv()
                    at = half_rows(m, near[1 - h], h)
                    g_all[m][at] = (
                        g_all[m][at].astype(F32) + e_all[m][l, h].astype(F32)
                    ).astype(BF16)
                    b_copy(l, m, 1 - h).start()

        def share_drain(l, m):
            for q in range(chips):
                c_copy(l, m, q).wait_send()
            if square:
                for t in range(2):
                    e_copy(l, m, t, far).wait_send()
                    b_copy(l, m, t).wait_send()
            else:
                for t in range(chips - 1):
                    h_copy(l, m, t).wait_send()
            own_out(l, m).wait()

        def share_end(l, m):
            if square:
                for t in range(2):
                    b_copy(l, m, t).wait_recv()
            else:
                for t in range(chips - 1):
                    h_copy(l, m, t).wait_recv()

        def dkv_copy(l, s, d):
            return remote(
                dkv_out.at[d - 1, srow(s)], dkv_in.at[l, d - 1, srow(s)],
                dsend.at[l, d - 1, s], drecv.at[l, d - 1, s],
                device_at("ctx", lax.rem(here + ctx_count - d, ctx_count)),
            )

        def dkv_drain(l):
            for s in range(seqs):
                for d in range(1, back + 1):
                    @pl.when(here - d >= 0)
                    def _():
                        dkv_copy(l, s, d).wait_send()

        def add_term(r, value):
            term[r : r + 1, :] = term[r : r + 1, :] + value

        def unit_steps(l, s):
            last = l == layers - 1

            def cast():
                value = go_ref[srow(s)].astype(F32) if last else gy[srow(s)]
                if last:
                    gy[srow(s)] = value
                gyb[srow(s)] = value.astype(BF16)
                add_term(bias_row(l, 5), colsum(value))

            def tile(t):
                off = slice(t * 256, (t + 1) * 256)
                dup = nn(gyb[srow(s)], wd[l, :, off]) * gs[l, srow(s), off]
                row = pl.ds(bias_row(l, 6) + me, 1)
                term[row, off] = term[row, off] + colsum(dup)
                dub[srow(s), off] = dup.astype(BF16)

            return [cast] + [lambda t=t: tile(t) for t in range(ffc // 256)]

        def second_back(l):
            def consumer(c, total):
                normed, inverse = norm_parts(x2[l, crow(c)])
                add_term(gain_row(l, 1), colsum(total * normed))
                add_term(bias_row(l, 1), colsum(total))
                value = gy[crow(c)] + norm_back(total, normed, inverse, vrow(gain_row(l, 1)))
                add_term(bias_row(l, 4), colsum(value))
                gy[crow(c)] = value
                gxb[crow(c)] = value.astype(BF16)

            return consumer

        def first_back(l):
            def consumer(c, total):
                base = x0_ref[crow(c)].astype(F32) if l == 0 else x1[crow(c)]
                normed, inverse = norm_parts(base)
                add_term(gain_row(l, 0), colsum(total * normed))
                add_term(bias_row(l, 0), colsum(total))
                value = gy[crow(c)] + norm_back(total, normed, inverse, vrow(gain_row(l, 0)))
                if l == 0:
                    gin_ref[crow(c)] = value.astype(BF16)
                else:
                    gy[crow(c)] = value

            return consumer

        def attend_back_steps(l, s):
            deltas = []

            def begin():
                dctx[srow(s)] = nn(gxb[srow(s)], wo[l]).astype(BF16)
                stacked(qst, qkv[l, srow(s), :cols] * BF16(scale))
                stacked(dst, dctx[srow(s), :])
                product = dctx[srow(s), :].astype(F32) * ctxs[l, srow(s)].astype(F32)
                for h in range(heads):
                    deltas.append(
                        jnp.sum(jnp.where(head_lanes[h], product, 0.0), -1, keepdims=True)
                    )

            def block(d):
                keys, values = key_block(l, s, d)
                score = nt(qst[...], keys)
                gprob = nt(dst[...], values)
                mask, dist = block_mask(s, d), block_dist(d)
                probs, gscores = [], []
                for h in range(heads):
                    hrow = slice(h * rows, (h + 1) * rows)
                    raw = score[hrow] - slopes[h] * dist - lse[l * seqs + s, hrow, :]
                    prob = jnp.where(mask, jnp.exp(jnp.where(mask, raw, 0.0)), 0.0)
                    probs.append(prob.astype(BF16))
                    gscores.append((prob * (gprob[hrow] - deltas[h])).astype(BF16))
                probs = jnp.concatenate(probs, 0)
                gscores = jnp.concatenate(gscores, 0)
                gkeys = tn(gscores, qst[...])
                gvalues = tn(probs, dst[...])
                if d:
                    dkv_out[d - 1, srow(s), :cols] = gkeys.astype(BF16)
                    dkv_out[d - 1, srow(s), cols:] = gvalues.astype(BF16)

                    @pl.when(here - d >= 0)
                    def _():
                        dkv_copy(l, s, d).start()
                else:
                    dkv0[srow(s), :cols] = gkeys
                    dkv0[srow(s), cols:] = gvalues
                step = nn(gscores, keys)
                acc[...] = step if d == back else acc[...] + step

            def close():
                out = jnp.zeros((rows, cols), F32)
                for h in range(heads):
                    out = jnp.where(head_lanes[h], acc[h * rows : (h + 1) * rows, :], out)
                out = out * scale
                r = bias_row(l, 2)
                term[r : r + 1, mine] = term[r : r + 1, mine] + colsum(out)
                dqkv[srow(s), :cols] = out.astype(BF16)

            return [begin] + [lambda d=d: block(d) for d in range(back, -1, -1)] + [close]

        def gather_dkv(l, s):
            for d in range(back, 0, -1):
                @pl.when(here + d < ctx_count)
                def _():
                    dkv_copy(l, s, d).wait_recv()
                    dkv0[srow(s), :] = dkv0[srow(s), :] + dkv_in[l, d - 1, srow(s)].astype(F32)
            r = bias_row(l, 3)
            term[r : r + 1, mine] = term[r : r + 1, mine] + colsum(dkv0[srow(s), cols:])
            dqkv[srow(s), cols:] = dkv0[srow(s), :].astype(BF16)

        def in_product_steps(p, l, s):
            def tile(t):
                off = slice(t * 256, (t + 1) * 256)
                value = nt(dqkv[srow(s), :cols], wq[l, 0, off, :])
                for u in (1, 2):
                    value = value + nt(dqkv[srow(s), u * cols : (u + 1) * cols], wq[l, u, off, :])
                part_b[p, srow(s), off] = value.astype(BF16)

            return [lambda t=t: tile(t) for t in range(width // 256)]

        def grad_tiles(one):
            return [lambda c=c: one(slice(c * LANES, (c + 1) * LANES)) for c in range(tiles)]

        def backward_layer(l, before):
            last = l == layers - 1

            def down_grads(off):
                gd[off] = tn(gyb[:, off], act[l]).astype(BF16)

            def up_grads(off):
                gu[off] = tn(a2[l, :, off], dub[...]).astype(BF16)

            def out_grads(off):
                gw[off] = tn(gxb[:, off], ctxs[l]).astype(BF16)

            def in_grads(off):
                for u in range(3):
                    gq[u, off] = tn(
                        a1[l, :, off], dqkv[:, u * cols : (u + 1) * cols]
                    ).astype(BF16)

            host, late = before
            p = sum_begin(first)
            steps = unit_steps(l, first)
            steps += product_steps(p, first, lambda: dub[srow(first)], lambda off: wu[l, off, :])
            weave(steps, host, 3 if last else 1)
            sum_start(p, first)
            finish(host)
            finish(late)
            early, wait, host, late = sum_plan(p, second_back(l))
            sum_begin(second)
            steps = unit_steps(l, second)
            steps += product_steps(p, second, lambda: dub[srow(second)], lambda off: wu[l, off, :])
            weave(steps, early, len(steps) - 3)
            sum_start(p, second)
            finish(early)
            fillers = []
            if not last:
                share_drain(l + 1, 2)
                share_drain(l + 1, 3)
                relays = [lambda: share_relay(l + 1, 0), lambda: share_relay(l + 1, 1)]
                fillers += share_chip_steps(l + 1, 0) + share_chip_steps(l + 1, 1)
            else:
                relays = []
            fillers += grad_tiles(down_grads) + [lambda: share_core(l, 3)]
            fillers += relays + grad_tiles(up_grads) + [lambda: share_core(l, 2)]
            finish(wait, fillers)
            if not last:
                dkv_drain(l + 1)
            weave(attend_back_steps(l, first), host)
            finish(host, fillers)
            finish(late, fillers)
            run_steps(fillers)
            steps = attend_back_steps(l, second)
            steps[-2:] = share_chip_steps(l, 3) + steps[-2:] + share_chip_steps(l, 2)
            run_steps(steps)
            if not last:
                share_drain(l + 1, 0)
                share_drain(l + 1, 1)
            gather_dkv(l, first)
            p = sum_begin(first)
            run_steps(in_product_steps(p, l, first))
            sum_start(p, first)
            share_relay(l, 3)
            early, wait, host, late = sum_plan(p, first_back(l))
            gather_dkv(l, second)
            sum_begin(second)
            steps = in_product_steps(p, l, second)
            weave(steps, early, len(steps) - 2)
            sum_start(p, second)
            finish(early)
            fillers = [lambda: share_relay(l, 2)] + grad_tiles(out_grads) + [lambda: share_core(l, 1)]
            fillers += grad_tiles(in_grads) + [lambda: share_core(l, 0)]
            finish(wait, fillers, 2)
            run_steps(fillers)
            if l:
                return host, late
            fillers = share_chip_steps(0, 1) + share_chip_steps(0, 0)
            fillers += [lambda: share_relay(0, 1), lambda: share_relay(0, 0)]
            finish(host, fillers)
            finish(late, fillers)
            run_steps(fillers)

        for l in reversed(range(layers)):
            carried = backward_layer(l, carried)

        alike = [gain_row(l, i) for l in range(layers) for i in range(2)] + [
            bias_row(l, j) for l in range(layers) for j in (0, 1, 4, 5)
        ]

        @pl.when(me != 0)
        def _():
            for r in alike:
                term[r : r + 1, :] = jnp.zeros((1, width), F32)

        def t1_copy(t, g):
            to = lax.rem(rank + t + 1, owners)
            tile = pl.ds(pl.multiple_of((to // group) * LANES, LANES), LANES)
            return remote(term.at[:, tile], tland.at[g], t1send.at[t], t1recv.at[t], plane[t])

        def t2_copy(t):
            return remote(tsum, tz.at[t], t2send.at[t], t2recv.at[t], zpeers[t])

        for t in range(owners - 1):
            t1_copy(t, rank).start()
        own_tile = pl.ds(pl.multiple_of((rank // group) * LANES, LANES), LANES)
        total = term[:, own_tile]
        for t in range(owners - 1):
            source = lax.rem(rank + owners - 1 - t, owners)
            t1_copy(t, source).wait_recv()
            total = total + tland[source]
        tsum[...] = total
        for t in range(mp_count - 1):
            t2_copy(t).start()
        for t in range(mp_count - 1):
            t2_copy(t).wait_recv()
            total = total + tz[t]
        total = pltpu.roll(total, lax.rem(LANES - offset, LANES), 1)
        for l in range(layers):
            gain_out[l] = total[l * 2 : l * 2 + 2, :part]
            low = layers * 2 + l * 10
            bias_out[l] = total[low : low + 10, :part]

        for m in range(4):
            share_drain(0, m)
            for l in range(layers):
                share_end(l, m)
                w_sent(l, m)
                for t in range(chips):
                    f_copy(l, m, t, rank).wait_send()
        dkv_drain(0)
        sum_drain(0, 0, tokens // CHUNK)
        sum_drain(1, 0, tokens // CHUNK)
        for t in range(mp_count - 1):
            vz_copy(t).wait_send()
            t2_copy(t).wait_send()
        for t in range(owners - 1):
            v2_copy(t, rank).wait_send()
            t1_copy(t, rank).wait_send()
        for d in range(1, back + 1):
            @pl.when(here + d < ctx_count)
            def _():
                seg_copy(d).wait_send()
                for l in range(layers):
                    for s in range(seqs):
                        kv_copy(l, s, d).wait_send()

    def vm(*shape, dtype=BF16):
        return pltpu.VMEM(shape, dtype)

    def dma(*shape):
        return pltpu.SemaphoreType.DMA(shape)

    scratch = [vm(layers, 3, width, cols)] + [vm(layers, width, n) for n in sizes[1:]]
    scratch += [
        vm(tokens, width, dtype=F32),
        vm(layers, tokens, width, dtype=F32),
        vm(layers, tokens, width),
        vm(layers, tokens, 3 * cols),
        vm(layers, back, tokens, 2 * cols),
        vm(layers, tokens, cols),
        vm(layers * seqs, stack, 1, dtype=F32),
        vm(layers, tokens, width),
        vm(layers, tokens, ffc, dtype=F32),
        vm(layers, tokens, ffc),
    ]
    scratch += [vm(2, tokens, width)] * 5
    scratch += [
        vm(tokens, width, dtype=F32),
        vm(tokens, width),
        vm(tokens, width),
        vm(tokens, ffc),
        vm(tokens, cols),
        vm(tokens, 3 * cols),
        vm(tokens, 2 * cols, dtype=F32),
        vm(back, tokens, 2 * cols),
        vm(layers, back, tokens, 2 * cols),
    ]
    scratch += [vm(3, width, cols)] + [vm(width, n) for n in sizes[1:]]
    scratch += [vm(layers, 3, width // 2, cols)]
    scratch += [vm(layers, width // 2, n) for n in sizes[1:]]
    half = piece // 2 if chips == 4 and piece % 32 == 0 else 16
    scratch += [vm(layers, 2, 3, half, cols)] + [vm(layers, 2, half, n) for n in sizes[1:]]
    scratch += [
        vm(VEC_ROWS, LANES, dtype=F32),
        vm(VEC_ROWS, LANES),
        vm(seqs, rows, rows, dtype=F32),
        vm(mp_count - 1, VEC_ROWS, LANES),
        vm(owners, VEC_ROWS, LANES),
        vm(VEC_ROWS, LANES),
        vm(VEC_ROWS, width, dtype=F32),
        vm(back, seqs, rows, dtype=jnp.int32),
        vm(VEC_ROWS, width, dtype=F32),
        vm(owners, VEC_ROWS, LANES, dtype=F32),
        vm(VEC_ROWS, LANES, dtype=F32),
        vm(mp_count - 1, VEC_ROWS, LANES, dtype=F32),
        vm(stack, cols, dtype=F32),
        vm(stack, cols),
        vm(stack, cols),
    ]
    scratch += [
        dma(layers, 4),
        dma(layers, 4, max(4, chips)), dma(layers, 4, max(4, chips)),
        dma(layers, 4, chips), dma(layers, 4, chips),
        dma(2, chunks), dma(2, chunks), dma(2, chunks), dma(2, chunks),
        dma(mp_count - 1), dma(mp_count - 1),
        dma(owners - 1), dma(owners - 1),
        dma(layers + 1, back, seqs), dma(layers + 1, back, seqs),
        dma(1), dma(1),
        dma(layers, back, seqs), dma(layers, back, seqs),
        dma(layers, 4, chips), dma(layers, 4, chips),
        dma(layers, 4, max(4, chips)), dma(layers, 4, max(4, chips)),
        dma(layers, 4),
        dma(owners - 1), dma(owners - 1),
        dma(mp_count - 1), dma(mp_count - 1),
    ]
    return pl.pallas_call(
        kernel,
        out_shape=[
            jax.ShapeDtypeStruct((tokens, width), BF16),
            jax.ShapeDtypeStruct((tokens, width), BF16),
            jax.ShapeDtypeStruct((layers, 2, part), F32),
            jax.ShapeDtypeStruct((layers, 10, part), F32),
        ]
        + [jax.ShapeDtypeStruct((3 if chips == 4 and piece % 32 == 0 else chips,) + w.shape, BF16) for w in weights],
        in_specs=[VMEM] * 5 + [ANY] * 4,
        out_specs=[VMEM] * 4 + [ANY] * 4,
        scratch_shapes=scratch,
        compiler_params=pltpu.CompilerParams(
            collective_id=0, has_side_effects=True, vmem_limit_bytes=62 * 1024 * 1024
        ),
        name="both_layers",
    )(x0, gout, seg, gains, biases, *weights)


def per_device(hidden_in, segment_ids, gains, biases, w_qkv, w_out_t, w_up, w_down_t, grad_out):
    seqs, rows, width = hidden_in.shape
    layers = w_qkv.shape[0]
    cols = w_qkv.shape[3]
    ffc = w_up.shape[2]
    piece = w_qkv.shape[1]
    part = gains.shape[2]
    ctx_count = lax.axis_size("ctx")
    mp_count = lax.axis_size("mp")
    owners = lax.axis_size("batch") * ctx_count
    dims = (layers, seqs, rows, width, cols, ffc, part, owners, ctx_count, mp_count)
    output, grad_in, grad_gains, grad_biases, gq, go, gu, gd = run_all(
        hidden_in.reshape(seqs * rows, width),
        grad_out.reshape(seqs * rows, width),
        segment_ids, gains, biases,
        [jnp.transpose(w_qkv, (0, 2, 1, 3)), w_out_t, w_up, w_down_t],
        dims,
    )
    def total(slots):
        acc = slots[0].astype(F32)
        for t in range(1, slots.shape[0]):
            acc = acc + slots[t].astype(F32)
        return acc

    return (
        output.reshape(hidden_in.shape),
        grad_in.reshape(hidden_in.shape),
        grad_gains,
        grad_biases,
        jnp.transpose(total(gq), (0, 2, 1, 3)),
        total(go),
        total(gu),
        total(gd),
    )


def solution(mesh):
    in_specs = (
        P("batch", "ctx", None),
        P("batch", "ctx"),
        P(None, None, ("batch", "ctx", "mp")),
        P(None, None, ("batch", "ctx", "mp")),
        P(None, ("batch", "ctx"), None, "mp"),
        P(None, ("batch", "ctx"), "mp"),
        P(None, ("batch", "ctx"), "mp"),
        P(None, ("batch", "ctx"), "mp"),
        P("batch", "ctx", None),
    )
    out_specs = (
        P("batch", "ctx", None),
        P("batch", "ctx", None),
        P(None, None, ("batch", "ctx", "mp")),
        P(None, None, ("batch", "ctx", "mp")),
        P(None, ("batch", "ctx"), None, "mp"),
        P(None, ("batch", "ctx"), "mp"),
        P(None, ("batch", "ctx"), "mp"),
        P(None, ("batch", "ctx"), "mp"),
    )
    return jax.shard_map(
        per_device, mesh=mesh, in_specs=in_specs, out_specs=out_specs, check_vma=False
    )
```
